256 devices in a mesh: dp: 8 (over x, core), expert: 32 (over y, z).
Axes of the slice: x: 4, y: 4, z: 8, core: 2. Of those that a mesh axis runs over, the one named last changes fastest.
Arguments:
- tokens: bfloat16 [8192, 3584], P(('dp', 'expert')), may hold values from -6 to 6
- expert_ids: int32 [8192, 2], P(('dp', 'expert')), may hold values from 0 to 31, all different within a row; in each aligned block of 32 rows (0 to 31, 32 to 63, ...) at most 3 rows name the same one
- mix_weights: float32 [8192, 2], P(('dp', 'expert')), may hold values from 0.25 to 1
- w_up: bfloat16 [32, 3584, 3072], P('expert', None, 'dp'), may hold values from -0.09375 to 0.09375
- w_down: bfloat16 [32, 3072, 3584], P('expert', 'dp'), may hold values from -0.109375 to 0.109375
- out_grad: bfloat16 [8192, 3584], P(('dp', 'expert')), may hold values from -3 to 3
Outputs:
- layer_out: bfloat16 [8192, 3584], P(('dp', 'expert'))
- token_grad: bfloat16 [8192, 3584], P(('dp', 'expert'))
- up_grad: bfloat16 [32, 3584, 3072], P('expert', None, 'dp')
- down_grad: bfloat16 [32, 3072, 3584], P('expert', 'dp')
The draws below stay inside these ranges and needn't reach their ends.
Inputs may be any that keep to these rules, and one draw needn't show every extreme that they name: `expert_ids`: the two experts of a token differ. The 32 tokens of one device name one expert at most 3 times, and in every draw some device names some expert exactly 3 times.
All inputs are finite; a program needn't handle non-finite values.
Results may differ from the reference program's by a relative error of at most 0.015.
Values may be sent and summed in bfloat16 or wider, within the bound.
No kernel may reach another device: no remote copies, remote signals or barrier semaphores. Data moves between devices by JAX's collectives and lax.ppermute only.
A program may use at most 128 MiB of HBM per device.

```python
import math
import jax
import jax.numpy as jnp
import numpy as np
from jax import lax

D = 3584
FF = 3072
TOK_DEV = 32
EXPERTS = 32
CAP = 3
TOKENS = 8192
N_DP = 8
N_EXPERT = 32


def block_scale(own_key, extent, shards, smallest, largest):
    loudness, own = 1.0, jax.random.fold_in(own_key, 6)
    for dim, parts in shards:
        heights = jnp.exp(jax.random.uniform(jax.random.fold_in(own, dim), (parts,), jnp.float32, smallest / len(shards), largest / len(shards)))
        loudness = loudness * jnp.repeat(heights, extent[dim] // parts).reshape([-1 if axis == dim else 1 for axis in range(len(extent))])
    return loudness


def deal_out(rng, own, number, rows, count, top, bound, skew):
    sequence = jax.random.permutation(rng, count)
    packed, ordinary = load_shares(count, rows * top, bound, skew, True), load_shares(count, rows * top, bound, skew, False)
    places = jnp.arange(count)

    def named(lengths, rotation):
        used = int((lengths > 0).sum())
        fixed = max(1, used // 4)
        shifted = fixed + (places - fixed + rotation * (used - fixed)) % max(1, count - fixed)
        return jnp.zeros((count,), jnp.int32).at[sequence[jnp.where(places < fixed, places, shifted)]].set(jnp.asarray(lengths, jnp.int32))

    lengths = jnp.where(number % 4 == 0, named(packed, number // 4), named(ordinary, number - number // 4 - 1))
    mixed = jax.random.permutation(jax.random.fold_in(own, 3), count)
    donor, taker = mixed[0:count // 2 * 2:2], mixed[1:count // 2 * 2:2]
    margin = jnp.minimum(lengths[donor] - 1, bound - lengths[taker]) // 2
    margin = jnp.where((donor == sequence[0]) | (taker == sequence[0]) | (lengths[taker] == 0), 0, jnp.maximum(margin, 0))
    shifted = jax.random.randint(jax.random.fold_in(own, 4), (count // 2,), 0, 1 << 20) % (margin + 1)
    lengths = lengths.at[donor].add(-shifted).at[taker].add(shifted)
    labels = jnp.searchsorted(jnp.cumsum(lengths), jnp.arange(rows * top), side="right").astype(jnp.int32)
    grid = labels.reshape(top, rows).T
    grid = grid[jax.random.permutation(jax.random.fold_in(own, 1), rows)]
    rotation = jax.random.randint(jax.random.fold_in(own, 2), (rows, 1), 0, top)
    return jnp.take_along_axis(grid, (jnp.arange(top)[None, :] + rotation) % top, axis=1)


def load_shares(number_of, total, most, slope, full):
    portions = [(1 << 20) // math.isqrt(standing ** slope) + 1 for standing in range(1, number_of + 1)]
    largest = most if full else min(most, max(-(-total // number_of), total * portions[0] // sum(portions)))
    least = 1 if total - largest >= number_of - 1 else 0
    given, surplus = [largest] + [least] * (number_of - 1), total - largest - least * (number_of - 1)
    while surplus > 0:
        candidates = [i for i in range(1, number_of) if given[i] < largest] or [i for i in range(1, number_of) if given[i] < most]
        mass, budget = sum([portions[i] for i in candidates]), surplus
        for i in candidates:
            addition = min(most - given[i], max(1, budget * portions[i] // mass), surplus)
            given[i] = given[i] + addition
            surplus = surplus - addition
    return np.array(given)


def gaussian(key, extent, deviation, most, pieces=(), kind=jnp.bfloat16):
    entries = deviation * jax.random.normal(key, extent, jnp.float32)
    if pieces:
        entries = entries * block_scale(key, extent, pieces, -0.22, 0.18)
    return jnp.clip(entries, -most, most).astype(kind)


def setup_inputs(seed: int = 0) -> dict:
    keys = jax.random.split(jax.random.key(seed), 7)
    tokens = gaussian(keys[0], (TOKENS, D), 1.0, 6.0, ((0, 256),))
    expert_ids_keys = jax.random.split(jax.random.fold_in(keys[1], 1), TOKENS // TOK_DEV)
    expert_ids_turns = jax.random.permutation(jax.random.fold_in(keys[1], 3), TOKENS // TOK_DEV)
    expert_ids = jax.vmap(lambda own, number: deal_out(jax.random.fold_in(keys[1], 2), own, number, TOK_DEV, EXPERTS, 2, CAP, 2))(expert_ids_keys, expert_ids_turns).reshape((TOKENS, 2))
    mix_weights = jnp.clip(0.25 + 0.75 * jax.random.uniform(keys[2], (TOKENS, 2), jnp.float32) ** block_scale(keys[2], (TOKENS, 2), ((0, 256),), -0.2, 0.2), 0.25, 1.0)
    w_up = gaussian(keys[3], (EXPERTS, D, FF), D ** -0.5, 0.09375, ((0, 32), (2, 8)))
    w_down = gaussian(keys[4], (EXPERTS, FF, D), FF ** -0.5, 0.109375, ((0, 32), (1, 8)))
    out_grad = gaussian(keys[5], (TOKENS, D), 0.5, 3.0, ((0, 256),))
    return dict(tokens=tokens, expert_ids=expert_ids, mix_weights=mix_weights, w_up=w_up, w_down=w_down, out_grad=out_grad)


def reference(tokens, expert_ids, mix_weights, w_up, w_down, out_grad):
    row_bound = N_DP * N_EXPERT * CAP
    block_width = FF // N_DP
    pair_ids = expert_ids.reshape(-1)
    pair_weights = mix_weights.reshape(-1).astype(jnp.float32)

    def per_expert(carry, expert):
        out_total, grad_total = carry
        hits = pair_ids == expert
        chosen = jnp.nonzero(hits, size=row_bound, fill_value=0)[0].astype(jnp.int32)
        live = jnp.arange(row_bound, dtype=jnp.int32) < jnp.sum(hits.astype(jnp.int32))
        token_index = (chosen // 2).astype(jnp.int32)
        weight = jnp.where(live, pair_weights[chosen], jnp.zeros((), jnp.float32))
        rows = jnp.where(live[:, None], tokens[token_index], jnp.zeros((), tokens.dtype))
        up_matrix = w_up[expert]
        down_matrix = w_down[expert]
        pre_act = jnp.dot(rows, up_matrix, preferred_element_type=jnp.float32)
        squash = jax.nn.sigmoid(pre_act)
        hidden = (pre_act * squash).astype(jnp.bfloat16)
        block_parts = jnp.einsum("rnk,nkd->rnd", hidden.reshape(row_bound, N_DP, block_width).astype(jnp.float32), down_matrix.reshape(N_DP, block_width, D).astype(jnp.float32))
        rounded = lax.optimization_barrier(block_parts.astype(jnp.bfloat16))
        expert_out = jnp.sum(rounded.astype(jnp.float32), axis=1).astype(jnp.bfloat16)
        out_total = out_total.at[token_index].add(weight[:, None] * expert_out.astype(jnp.float32))
        out_scaled = (weight[:, None] * out_grad[token_index].astype(jnp.float32)).astype(jnp.bfloat16)
        hidden_grad = jnp.dot(out_scaled, down_matrix.T, preferred_element_type=jnp.float32)
        down_part = jnp.dot(hidden.T, out_scaled, preferred_element_type=jnp.float32).astype(jnp.bfloat16)
        pre_grad = (hidden_grad * squash * (1.0 + pre_act * (1.0 - squash))).astype(jnp.bfloat16)
        up_part = jnp.dot(rows.T, pre_grad, preferred_element_type=jnp.float32).astype(jnp.bfloat16)
        grad_parts = jnp.einsum("rnk,dnk->rnd", pre_grad.reshape(row_bound, N_DP, block_width).astype(jnp.float32), up_matrix.reshape(D, N_DP, block_width).astype(jnp.float32))
        grad_rounded = lax.optimization_barrier(grad_parts.astype(jnp.bfloat16))
        pair_grad = jnp.sum(grad_rounded.astype(jnp.float32), axis=1).astype(jnp.bfloat16)
        grad_total = grad_total.at[token_index].add(pair_grad.astype(jnp.float32))
        return (out_total, grad_total), (up_part, down_part)

    start_state = (jnp.zeros((TOKENS, D), jnp.float32), jnp.zeros((TOKENS, D), jnp.float32))
    (out_total, grad_total), (up_grad, down_grad) = lax.scan(per_expert, start_state, jnp.arange(EXPERTS, dtype=jnp.int32))
    return (out_total.astype(jnp.bfloat16), grad_total.astype(jnp.bfloat16), up_grad, down_grad)
```

```python
import jax
import jax.numpy as jnp
from jax import lax
from jax.sharding import PartitionSpec as P


def per_device(tokens, expert_ids, mix_weights, w_up, w_down, out_grad):
    tok_count, width = tokens.shape
    dp_count = lax.axis_size("dp")
    ring = dp_count // 2
    expert_count = lax.axis_size("expert") * w_up.shape[0]
    capacity = max(2, 3 * tok_count // expert_count)
    slot_count = expert_count * capacity

    def x_perm(step):
        return [(2 * x + c, 2 * ((x + step) % ring) + c) for x in range(ring) for c in range(2)]

    core_perm = [(i, i ^ 1) for i in range(dp_count)]

    def x_shift(value, step):
        return lax.ppermute(value, "dp", x_perm(step % ring))

    def core_swap(value):
        return lax.ppermute(value, "dp", core_perm)

    def exchange(value):
        return lax.all_to_all(value, "expert", split_axis=0, concat_axis=0, tiled=True)

    def dot(a, b, dims):
        return lax.dot_general(a, b, (dims, ((), ())), preferred_element_type=jnp.float32)

    up_own, down_own = w_up[0], w_down[0]
    up_chip = jnp.concatenate([up_own, core_swap(up_own)], axis=1)
    down_chip = jnp.concatenate([down_own, core_swap(down_own)], axis=0)
    units = up_own.shape[1]

    one_hot = (
        expert_ids[:, :, None] == jnp.arange(expert_count, dtype=jnp.int32)[None, None, :]
    ).astype(jnp.int32)
    pair_hits = one_hot.reshape(tok_count * 2, expert_count)
    before = jnp.cumsum(pair_hits, axis=0) - pair_hits
    position = jnp.sum(before * pair_hits, axis=1)
    target = expert_ids.reshape(-1) * capacity + position
    placing = (target[:, None] == jnp.arange(slot_count, dtype=jnp.int32)[None, :]).reshape(
        tok_count, 2, slot_count
    )
    select = jnp.sum(placing.astype(jnp.bfloat16), axis=1)
    weighting = jnp.sum(placing.astype(jnp.float32) * mix_weights[:, :, None], axis=1)
    token_send = dot(select, tokens, ((0,), (0,))).astype(jnp.bfloat16)
    grad_send = lax.dot_general(
        weighting,
        out_grad.astype(jnp.float32),
        (((0,), (0,)), ((), ())),
        precision=lax.Precision.HIGHEST,
    ).astype(jnp.bfloat16)

    def gather_x(own):
        return jnp.concatenate([own] + [x_shift(own, step) for step in range(1, ring)], axis=0)

    def scatter_x(rows):
        parts = jnp.split(rows, ring, axis=0)
        total = parts[0].astype(jnp.float32)
        for step in range(1, ring):
            total = total + x_shift(parts[step], -step).astype(jnp.float32)
        return total.astype(jnp.bfloat16)

    token_rows = gather_x(exchange(token_send))
    grad_rows = gather_x(exchange(grad_send))

    pre_act = dot(token_rows, up_chip, ((1,), (0,)))
    squash = jax.nn.sigmoid(pre_act)
    hidden = (pre_act * squash).astype(jnp.bfloat16)
    out_rows = scatter_x(dot(hidden, down_chip, ((1,), (0,))).astype(jnp.bfloat16))
    hidden_grad = dot(grad_rows, down_chip, ((1,), (1,)))
    slope = squash * (1.0 + pre_act * (1.0 - squash))
    pre_grad = (hidden_grad * slope).astype(jnp.bfloat16)
    in_rows = scatter_x(dot(pre_grad, up_chip, ((1,), (1,))).astype(jnp.bfloat16))
    out_back = exchange(out_rows)
    in_back = exchange(in_rows)

    hidden_all = jnp.concatenate([hidden[:, :units], core_swap(hidden[:, units:])], axis=0)
    pre_all = jnp.concatenate([pre_grad[:, :units], core_swap(pre_grad[:, units:])], axis=0)
    token_all = jnp.concatenate([token_rows, core_swap(token_rows)], axis=0)
    grad_all = jnp.concatenate([grad_rows, core_swap(grad_rows)], axis=0)
    grad_down = dot(hidden_all, grad_all, ((0,), (0,)))
    grad_up = dot(token_all, pre_all, ((0,), (0,)))

    layer_out = lax.dot_general(
        weighting,
        out_back.astype(jnp.float32),
        (((1,), (0,)), ((), ())),
        precision=lax.Precision.HIGHEST,
    ).astype(jnp.bfloat16)
    token_grad = dot(select, in_back, ((1,), (0,))).astype(jnp.bfloat16)
    return (
        layer_out,
        token_grad,
        grad_up.astype(jnp.bfloat16)[None],
        grad_down.astype(jnp.bfloat16)[None],
    )


def solution(mesh):
    rows = P(("dp", "expert"), None)
    up, down = P("expert", None, "dp"), P("expert", "dp", None)
    return jax.shard_map(
        per_device,
        mesh=mesh,
        in_specs=(rows, rows, rows, up, down, rows),
        out_specs=(rows, rows, up, down),
        check_vma=False,
    )
```

```python
import functools

import jax
import jax.numpy as jnp
from jax import lax
from jax.experimental import pallas as pl
from jax.experimental.pallas import tpu as pltpu
from jax.sharding import PartitionSpec as P


BF16, F32, I32 = jnp.bfloat16, jnp.float32, jnp.int32
STEPS = 2
CAP = 3
GROUP = 8


def dot(a, b, dims=((1,), (0,))):
    return lax.dot_general(a, b, (dims, ((), ())), preferred_element_type=F32)


def full(shape):
    return pl.BlockSpec(shape, lambda k: (0, 0))


def cost(flops, bytes_accessed):
    return pl.CostEstimate(flops=flops, transcendentals=0, bytes_accessed=bytes_accessed)


def gather_body(back, *refs):
    pieces, (w_own, w_other) = refs[:4], refs[4:6]
    if back:
        pre, (rows_out, first, second), (acc,) = refs[6], refs[7:10], refs[10:]
    else:
        rows_out, pre_out, first, second, acc = refs[6:]
    k = pl.program_id(0)
    size = pieces[0].shape[0]
    for b, piece in enumerate(pieces):
        rows_out[b * size : (b + 1) * size, :] = piece[...]
    if back:
        weight = jnp.concatenate([w_own[...], w_other[...]], axis=0)
        part = dot(rows_out[...], weight, ((1,), (1,)))
    else:
        weight = jnp.concatenate([w_own[...], w_other[...]], axis=1)
        part = dot(rows_out[...], weight)

    @pl.when(k == 0)
    def _():
        acc[...] = part

    @pl.when(k > 0)
    def _():
        acc[...] += part

    @pl.when(k == pl.num_programs(0) - 1)
    def _():
        units = first.shape[1]
        if back:
            pre_act = pre[...]
            squash = jax.nn.sigmoid(pre_act)
            value = (acc[...] * (squash * (1.0 + pre_act * (1.0 - squash)))).astype(BF16)
        else:
            pre_act = acc[...]
            pre_out[...] = pre_act
            value = (pre_act * jax.nn.sigmoid(pre_act)).astype(BF16)
        first[...] = value[:, :units]
        second[...] = value[:, units:]


def rows_matmul(pieces, w_own, w_other, pre, steps):
    back = pre is not None
    size, width = pieces[0].shape
    rows, cols = 4 * size, width // steps
    units = w_own.shape[0] if back else w_own.shape[1]
    piece = pl.BlockSpec((size, cols), lambda k: (0, k))
    weight = pl.BlockSpec((units, cols), lambda k: (0, k)) if back else pl.BlockSpec((cols, units), lambda k: (k, 0))
    wide, narrow = full((rows, 2 * units)), full((rows, units))
    narrow_shape = jax.ShapeDtypeStruct((rows, units), BF16)
    return pl.pallas_call(
        functools.partial(gather_body, back),
        grid=(steps,),
        in_specs=[piece] * 4 + [weight, weight] + [wide] * back,
        out_specs=[pl.BlockSpec((rows, cols), lambda k: (0, k))] + [wide] * (not back) + [narrow, narrow],
        out_shape=[jax.ShapeDtypeStruct((rows, width), BF16)]
        + [jax.ShapeDtypeStruct((rows, 2 * units), F32)] * (not back) + [narrow_shape, narrow_shape],
        scratch_shapes=[pltpu.VMEM((rows, 2 * units), F32)],
        cost_estimate=cost(4 * rows * width * units, 4 * (rows * width + width * units)),
    )(*pieces, w_own, w_other, *([pre] * back))


def project_body(by_rows, h_own, h_other, w_own, w_other, *outs):
    hidden = jnp.concatenate([h_own[...], h_other[...]], axis=1)
    if by_rows:
        weight = jnp.concatenate([w_own[...], w_other[...]], axis=1)
        value = dot(hidden, weight, ((1,), (1,))).astype(BF16)
    else:
        weight = jnp.concatenate([w_own[...], w_other[...]], axis=0)
        value = dot(hidden, weight).astype(BF16)
    size = outs[0].shape[0]
    for b, out in enumerate(outs):
        out[...] = value[b * size : (b + 1) * size, :]


def project(h_own, h_other, w_own, w_other, by_rows, steps):
    rows, units = h_own.shape
    width = w_own.shape[0] if by_rows else w_own.shape[1]
    cols, size = width // steps, rows // 4
    if by_rows:
        weight = pl.BlockSpec((cols, units), lambda k: (k, 0))
    else:
        weight = pl.BlockSpec((units, cols), lambda k: (0, k))
    return pl.pallas_call(
        functools.partial(project_body, by_rows),
        grid=(steps,),
        in_specs=[full((rows, units))] * 2 + [weight, weight],
        out_specs=[pl.BlockSpec((size, cols), lambda k: (0, k))] * 4,
        out_shape=[jax.ShapeDtypeStruct((size, width), BF16)] * 4,
        cost_estimate=cost(4 * rows * width * units, 2 * (rows * width + 2 * width * units)),
    )(h_own, h_other, w_own, w_other)


def down_grad_body(h_a, h_b, g_a, g_b, out):
    hidden = jnp.concatenate([h_a[...], h_b[...]], axis=0)
    rows = jnp.concatenate([g_a[...], g_b[...]], axis=0)
    out[...] = dot(hidden, rows, ((0,), (0,))).astype(BF16)


def down_grad(h_a, h_b, g_a, g_b, steps):
    rows, units = h_a.shape
    width = g_a.shape[1]
    cols = width // steps
    g_spec = pl.BlockSpec((rows, cols), lambda k: (0, k))
    return pl.pallas_call(
        down_grad_body,
        grid=(steps,),
        in_specs=[full((rows, units))] * 2 + [g_spec, g_spec],
        out_specs=pl.BlockSpec((units, cols), lambda k: (0, k)),
        out_shape=jax.ShapeDtypeStruct((units, width), BF16),
        cost_estimate=cost(4 * rows * width * units, 2 * (2 * rows * width + width * units)),
        name="wgrad_down",
    )(h_a, h_b, g_a, g_b)


def up_grad_body(t_a, t_b, p_a, p_b, out):
    rows = jnp.concatenate([t_a[...], t_b[...]], axis=0)
    pre = jnp.concatenate([p_a[...], p_b[...]], axis=0)
    out[...] = dot(rows, pre, ((0,), (0,))).astype(BF16)


def up_grad(t_a, t_b, p_a, p_b, steps):
    rows, units = p_a.shape
    width = t_a.shape[1]
    cols = width // steps
    t_spec = pl.BlockSpec((rows, cols), lambda k: (0, k))
    return pl.pallas_call(
        up_grad_body,
        grid=(steps,),
        in_specs=[t_spec, t_spec] + [full((rows, units))] * 2,
        out_specs=pl.BlockSpec((cols, units), lambda k: (k, 0)),
        out_shape=jax.ShapeDtypeStruct((width, units), BF16),
        cost_estimate=cost(4 * rows * width * units, 2 * (2 * rows * width + width * units)),
        name="wgrad_up",
    )(t_a, t_b, p_a, p_b)


def sizes(width):
    rest = 6 * (width // 28)
    return (width - rest) // 2, rest


def block_width(width):
    return sizes(width)[0]


def placements(row, base, slot):
    main = [row == base + 2 * slot, row == base + 2 * slot + 1]
    rest = ((slot == 0) & (row == base + 6)) | ((slot == 1) & (row == base + 7))
    last = [(slot == 2) & (row == base + 6), (slot == 2) & (row == base + 7)]
    return [hit.astype(BF16) for hit in (main[0], main[1], rest, last[0], last[1])]


def write_blocks(out, place, rows):
    wide, rest = sizes(rows.shape[1])
    half, start = rest // 2, 2 * wide
    lead = jnp.concatenate(place[:3], axis=1)
    second = jnp.concatenate(place[:2] + place[3:], axis=1)
    third = jnp.concatenate(place[:2], axis=1)
    out[:, :rest] = dot(lead, jnp.concatenate(
        [rows[:, :rest], rows[:, wide : wide + rest], rows[:, start:]], axis=0)).astype(BF16)
    end = rest + half
    out[:, rest:end] = dot(second, jnp.concatenate(
        [rows[:, rest:end], rows[:, wide + rest : wide + end],
         rows[:, start : start + half], rows[:, start + half :]], axis=0)).astype(BF16)
    out[:, end:] = dot(third, jnp.concatenate(
        [rows[:, end:wide], rows[:, wide + end : start]], axis=0)).astype(BF16)


def read_blocks(out, place, block, precision=None):
    wide, rest = sizes(out.shape[1])
    half, start = rest // 2, 2 * wide

    def pick(a, b):
        return lax.dot_general(
            a, b, (((1,), (0,)), ((), ())), precision=precision, preferred_element_type=F32)

    out[:, :wide] = pick(place[0], block).astype(BF16)
    out[:, wide:start] = pick(place[1], block).astype(BF16)
    both = jnp.concatenate([place[2], place[3]], axis=1)
    other = jnp.concatenate([place[2], place[4]], axis=1)
    side = block[:, rest : rest + half]
    out[:, start : start + half] = pick(
        both, jnp.concatenate([block[:, :half], side], axis=0)).astype(BF16)
    out[:, start + half :] = pick(
        other, jnp.concatenate([block[:, half:rest], side], axis=0)).astype(BF16)


def pair_slots(by_lane, by_row):
    count = by_lane.shape[1]
    same = by_lane == by_row
    first = lax.broadcasted_iota(I32, (count, count), 0)
    second = lax.broadcasted_iota(I32, (count, count), 1)
    along_lane = jnp.sum((same & (first < second)).astype(F32), axis=0, keepdims=True)
    along_row = jnp.sum((same & (second < first)).astype(F32), axis=1, keepdims=True)
    return along_lane.astype(I32), along_row.astype(I32)


def dispatch_body(scaled, ids_lane, ids_row, *refs):
    by_lane = ids_lane[...]
    slot, _ = pair_slots(by_lane, ids_row[...])
    out = refs[-1]
    row = lax.broadcasted_iota(I32, (out.shape[0], by_lane.shape[1]), 0)
    place = placements(row, by_lane * GROUP, slot)
    source = refs[-2][...]
    if scaled:
        source = source.astype(F32)
        mix = refs[0][...]
        pairs = [(mix[:, k : k + 1] * source).astype(BF16) for k in range(2)]
    else:
        pairs = [source, source]
    write_blocks(out, place, jnp.concatenate(pairs, axis=0))


def static_slots(axis, shape):
    index = lax.broadcasted_iota(I32, shape, axis)
    owner = (index * 43) >> 7
    return owner * GROUP, index - owner * CAP


def collect_body(left, middle, right, out):
    total = left[...].astype(F32) + middle[...].astype(F32) + right[...].astype(F32)
    rows = total.astype(BF16)
    shape = (out.shape[0], rows.shape[0])
    base, slot = static_slots(1, shape)
    write_blocks(out, placements(lax.broadcasted_iota(I32, shape, 0), base, slot), rows)


def unpack_body(block, out):
    shape = (out.shape[0], block.shape[0])
    base, slot = static_slots(0, shape)
    place = placements(lax.broadcasted_iota(I32, shape, 1), base, slot)
    read_blocks(out, place, block[...])


def combine_body(weighted, ids_lane, ids_row, *refs):
    block, out = refs[-2], refs[-1]
    by_row = ids_row[...]
    _, slot = pair_slots(ids_lane[...], by_row)
    shape = (by_row.shape[0], block.shape[0])
    place = placements(lax.broadcasted_iota(I32, shape, 1), by_row * GROUP, slot)
    count = out.shape[0]
    if weighted:
        mix = refs[0][...]
        place = [
            p[:count].astype(F32) * mix[:, 0:1] + p[count:].astype(F32) * mix[:, 1:2]
            for p in place
        ]
        read_blocks(out, place, block[...].astype(F32), lax.Precision.HIGHEST)
    else:
        read_blocks(out, [p[:count] + p[count:] for p in place], block[...])


def single(body, shape, flops, *args):
    moved = sum(a.size * a.dtype.itemsize for a in args) + 2 * shape[0] * shape[1]
    return pl.pallas_call(
        body, out_shape=jax.ShapeDtypeStruct(shape, BF16), cost_estimate=cost(flops, moved)
    )(*args)


def per_device(tokens, expert_ids, mix_weights, w_up, w_down, out_grad):
    tok_count, width = tokens.shape
    dp_count = lax.axis_size("dp")
    ring = dp_count // 2
    experts = lax.axis_size("expert") * w_up.shape[0]
    block_shape = (experts * GROUP, block_width(width))
    rows_shape = (experts * CAP, width)
    small = 2 * block_shape[0] * block_shape[1] * 256
    core_perm = [(i, i ^ 1) for i in range(dp_count)]

    def shift(value, step):
        perm = [(2 * x + c, 2 * ((x + step) % ring) + c) for x in range(ring) for c in range(2)]
        return lax.ppermute(value, "dp", perm)

    def swap(value):
        return lax.ppermute(value, "dp", core_perm)

    def exchange(packed):
        blocks = packed.reshape(experts, GROUP, block_shape[1])
        moved = lax.all_to_all(blocks, "expert", split_axis=0, concat_axis=0, tiled=True)
        return moved.reshape(block_shape)

    def small_call(body, shape, *args):
        return single(body, shape, small, *args)

    def gather_x(own, forward):
        left, right = shift(own, -1), shift(own, 1)
        relayed = right if forward == 1 else left
        return own, left, right, shift(relayed, forward)

    def scatter_x(parts, forward):
        own, left, right, far = parts
        via = shift(far, forward)
        if forward == 1:
            left = (left.astype(F32) + via.astype(F32)).astype(BF16)
        else:
            right = (right.astype(F32) + via.astype(F32)).astype(BF16)
        return own, shift(left, 1), shift(right, -1)

    up_own, down_own = w_up[0], w_down[0]
    by_choice = expert_ids.T
    ids_lane, ids_row = by_choice.reshape(1, -1), by_choice.reshape(-1, 1)

    token_send = small_call(
        functools.partial(dispatch_body, False), block_shape, ids_lane, ids_row, tokens)
    token_moved = exchange(token_send)
    grad_send = small_call(
        functools.partial(dispatch_body, True), block_shape,
        ids_lane, ids_row, mix_weights, out_grad)
    grad_moved = exchange(grad_send)

    up_other, down_other = swap(up_own), swap(down_own)
    token_own = small_call(unpack_body, rows_shape, token_moved)
    grad_own = small_call(unpack_body, rows_shape, grad_moved)
    token_parts = gather_x(token_own, 1)
    grad_parts = gather_x(grad_own, -1)

    token_rows, pre_act, h_own, h_other = rows_matmul(
        token_parts, up_own, up_other, None, STEPS)
    out_parts = project(h_own, h_other, down_own, down_other, False, STEPS)
    grad_rows, p_own, p_other = rows_matmul(
        grad_parts, down_own, down_other, pre_act, STEPS)
    in_parts = project(p_own, p_other, up_own, up_other, True, STEPS)

    out_send = small_call(collect_body, block_shape, *scatter_x(out_parts, 1))
    in_send = small_call(collect_body, block_shape, *scatter_x(in_parts, -1))
    out_back = exchange(out_send)
    in_back = exchange(in_send)

    h_in, g_in = swap(h_other), swap(grad_rows)
    p_in, t_in = swap(p_other), swap(token_rows)
    grad_down = down_grad(h_own, h_in, grad_rows, g_in, STEPS)
    grad_up = up_grad(token_rows, t_in, p_own, p_in, STEPS)

    layer_out = small_call(
        functools.partial(combine_body, True), (tok_count, width),
        ids_lane, ids_row, mix_weights, out_back)
    token_grad = small_call(
        functools.partial(combine_body, False), (tok_count, width),
        ids_lane, ids_row, in_back)
    return layer_out, token_grad, grad_up[None], grad_down[None]


def solution(mesh):
    rows = P(("dp", "expert"), None)
    up, down = P("expert", None, "dp"), P("expert", "dp", None)

    return jax.shard_map(
        per_device,
        mesh=mesh,
        in_specs=(rows, rows, rows, up, down, rows),
        out_specs=(rows, rows, up, down),
        check_vma=False,
    )
```

```python
import functools

import jax
import jax.numpy as jnp
from jax import lax
from jax.experimental import pallas as pl
from jax.experimental.pallas import tpu as pltpu
from jax.sharding import PartitionSpec as P


BF16, F32, I32 = jnp.bfloat16, jnp.float32, jnp.int32
STEPS = 2
CAP = 3
GROUP = 8


def dot(a, b, dims=((1,), (0,))):
    return lax.dot_general(a, b, (dims, ((), ())), preferred_element_type=F32)


def full(shape):
    return pl.BlockSpec(shape, lambda k: (0, 0))


def cost(flops, bytes_accessed):
    return pl.CostEstimate(flops=flops, transcendentals=0, bytes_accessed=bytes_accessed)


def gather_body(back, split, *refs):
    refs, pieces = list(refs), []
    for halves in split:
        pieces.append([refs.pop(0) for _ in range(halves)])
    w_own, w_other = refs[:2]
    if back:
        pre, rows_out, first, second, acc = refs[2:]
    else:
        rows_out, pre_out, first, second, acc = refs[2:]
    k = pl.program_id(0)
    size = pieces[0][0].shape[0]
    for b, piece in enumerate(pieces):
        for step in range(len(piece)):

            @pl.when((k == step) | (len(piece) == 1))
            def _():
                rows_out[b * size : (b + 1) * size, :] = piece[step][...]

    if back:
        weight = jnp.concatenate([w_own[...], w_other[...]], axis=0)
        part = dot(rows_out[...], weight, ((1,), (1,)))
    else:
        weight = jnp.concatenate([w_own[...], w_other[...]], axis=1)
        part = dot(rows_out[...], weight)

    @pl.when(k == 0)
    def _():
        acc[...] = part

    @pl.when(k > 0)
    def _():
        acc[...] += part

    @pl.when(k == pl.num_programs(0) - 1)
    def _():
        units = first.shape[1]
        if back:
            pre_act = pre[...]
            squash = jax.nn.sigmoid(pre_act)
            value = (acc[...] * (squash * (1.0 + pre_act * (1.0 - squash)))).astype(BF16)
        else:
            pre_act = acc[...]
            pre_out[...] = pre_act
            value = (pre_act * jax.nn.sigmoid(pre_act)).astype(BF16)
        first[...] = value[:, :units]
        second[...] = value[:, units:]


def rows_matmul(pieces, w_own, w_other, pre, steps):
    back = pre is not None
    split = tuple(len(piece) for piece in pieces)
    size, cols = pieces[-1][0].shape
    rows, width = 4 * size, cols * steps
    units = w_own.shape[0] if back else w_own.shape[1]
    whole, half = pl.BlockSpec((size, cols), lambda k: (0, k)), full((size, cols))
    piece_specs = [half if n > 1 else whole for n in split for _ in range(n)]
    weight = pl.BlockSpec((units, cols), lambda k: (0, k)) if back else pl.BlockSpec((cols, units), lambda k: (k, 0))
    wide, narrow = full((rows, 2 * units)), full((rows, units))
    narrow_shape = jax.ShapeDtypeStruct((rows, units), BF16)
    return pl.pallas_call(
        functools.partial(gather_body, back, split),
        grid=(steps,),
        in_specs=piece_specs + [weight, weight] + [wide] * back,
        out_specs=[pl.BlockSpec((rows, cols), lambda k: (0, k))] + [wide] * (not back) + [narrow, narrow],
        out_shape=[jax.ShapeDtypeStruct((rows, width), BF16)]
        + [jax.ShapeDtypeStruct((rows, 2 * units), F32)] * (not back) + [narrow_shape, narrow_shape],
        scratch_shapes=[pltpu.VMEM((rows, 2 * units), F32)],
        cost_estimate=cost(4 * rows * width * units, 4 * (rows * width + width * units)),
    )(*[part for piece in pieces for part in piece], w_own, w_other, *([pre] * back))


def project_body(by_rows, h_own, h_other, w_own, w_other, *outs):
    hidden = jnp.concatenate([h_own[...], h_other[...]], axis=1)
    if by_rows:
        weight = jnp.concatenate([w_own[...], w_other[...]], axis=1)
        value = dot(hidden, weight, ((1,), (1,))).astype(BF16)
    else:
        weight = jnp.concatenate([w_own[...], w_other[...]], axis=0)
        value = dot(hidden, weight).astype(BF16)
    size = outs[0].shape[0]
    for step in range(2):

        @pl.when(pl.program_id(0) == step)
        def _():
            for b in range(4):
                outs[2 * b + step][...] = value[b * size : (b + 1) * size, :]


def project(h_own, h_other, w_own, w_other, by_rows, steps):
    rows, units = h_own.shape
    width = w_own.shape[0] if by_rows else w_own.shape[1]
    cols, size = width // steps, rows // 4
    if by_rows:
        weight = pl.BlockSpec((cols, units), lambda k: (k, 0))
    else:
        weight = pl.BlockSpec((units, cols), lambda k: (0, k))
    return pl.pallas_call(
        functools.partial(project_body, by_rows),
        grid=(steps,),
        in_specs=[full((rows, units))] * 2 + [weight, weight],
        out_specs=[full((size, cols))] * 8,
        out_shape=[jax.ShapeDtypeStruct((size, cols), BF16)] * 8,
        cost_estimate=cost(4 * rows * width * units, 2 * (rows * width + 2 * width * units)),
    )(h_own, h_other, w_own, w_other)


def down_grad_body(h_a, h_b, g_a, g_b, out):
    hidden = jnp.concatenate([h_a[...], h_b[...]], axis=0)
    rows = jnp.concatenate([g_a[...], g_b[...]], axis=0)
    out[...] = dot(hidden, rows, ((0,), (0,))).astype(BF16)


def down_grad(h_a, h_b, g_a, g_b, steps):
    rows, units = h_a.shape
    width = g_a.shape[1]
    cols = width // steps
    g_spec = pl.BlockSpec((rows, cols), lambda k: (0, k))
    return pl.pallas_call(
        down_grad_body,
        grid=(steps,),
        in_specs=[full((rows, units))] * 2 + [g_spec, g_spec],
        out_specs=pl.BlockSpec((units, cols), lambda k: (0, k)),
        out_shape=jax.ShapeDtypeStruct((units, width), BF16),
        cost_estimate=cost(4 * rows * width * units, 2 * (2 * rows * width + width * units)),
        name="wgrad_down",
    )(h_a, h_b, g_a, g_b)


def up_grad_body(t_a, t_b, p_a, p_b, out):
    rows = jnp.concatenate([t_a[...], t_b[...]], axis=0)
    pre = jnp.concatenate([p_a[...], p_b[...]], axis=0)
    out[...] = dot(rows, pre, ((0,), (0,))).astype(BF16)


def up_grad(t_a, t_b, p_a, p_b, steps):
    rows, units = p_a.shape
    width = t_a.shape[1]
    cols = width // steps
    t_spec = pl.BlockSpec((rows, cols), lambda k: (0, k))
    return pl.pallas_call(
        up_grad_body,
        grid=(steps,),
        in_specs=[t_spec, t_spec] + [full((rows, units))] * 2,
        out_specs=pl.BlockSpec((cols, units), lambda k: (k, 0)),
        out_shape=jax.ShapeDtypeStruct((width, units), BF16),
        cost_estimate=cost(4 * rows * width * units, 2 * (2 * rows * width + width * units)),
        name="wgrad_up",
    )(t_a, t_b, p_a, p_b)


def sizes(width):
    rest = 6 * (width // 28)
    return (width - rest) // 2, rest


def block_width(width):
    return sizes(width)[0]


def placements(row, base, slot):
    main = [row == base + 2 * slot, row == base + 2 * slot + 1]
    rest = ((slot == 0) & (row == base + 6)) | ((slot == 1) & (row == base + 7))
    last = [(slot == 2) & (row == base + 6), (slot == 2) & (row == base + 7)]
    return [hit.astype(BF16) for hit in (main[0], main[1], rest, last[0], last[1])]


def write_blocks(out, place, rows):
    wide, rest = sizes(rows.shape[1])
    half, start = rest // 2, 2 * wide
    lead = jnp.concatenate(place[:3], axis=1)
    second = jnp.concatenate(place[:2] + place[3:], axis=1)
    third = jnp.concatenate(place[:2], axis=1)
    out[:, :rest] = dot(lead, jnp.concatenate(
        [rows[:, :rest], rows[:, wide : wide + rest], rows[:, start:]], axis=0)).astype(BF16)
    end = rest + half
    out[:, rest:end] = dot(second, jnp.concatenate(
        [rows[:, rest:end], rows[:, wide + rest : wide + end],
         rows[:, start : start + half], rows[:, start + half :]], axis=0)).astype(BF16)
    out[:, end:] = dot(third, jnp.concatenate(
        [rows[:, end:wide], rows[:, wide + end : start]], axis=0)).astype(BF16)


def read_blocks(width, place, block, parts=1):
    _, rest = sizes(width)
    half = rest // 2

    def pick(a, b):
        value = dot(a, b)
        size = value.shape[0] // parts
        total = value[(parts - 1) * size :]
        for part in range(parts - 2, -1, -1):
            total = total + value[part * size : (part + 1) * size]
        return total.astype(BF16)

    both = jnp.concatenate([place[2], place[3]], axis=1)
    other = jnp.concatenate([place[2], place[4]], axis=1)
    side = block[:, rest : rest + half]
    return jnp.concatenate(
        [
            pick(place[0], block),
            pick(place[1], block),
            pick(both, jnp.concatenate([block[:, :half], side], axis=0)),
            pick(other, jnp.concatenate([block[:, half:rest], side], axis=0)),
        ],
        axis=1,
    )


def pair_slots(by_lane, by_row):
    count = by_lane.shape[1]
    same = by_lane == by_row
    first = lax.broadcasted_iota(I32, (count, count), 0)
    second = lax.broadcasted_iota(I32, (count, count), 1)
    along_lane = jnp.sum((same & (first < second)).astype(F32), axis=0, keepdims=True)
    along_row = jnp.sum((same & (second < first)).astype(F32), axis=1, keepdims=True)
    return along_lane.astype(I32), along_row.astype(I32)


def dispatch_body(scaled, ids_lane, ids_row, *refs):
    by_lane = ids_lane[...]
    slot, _ = pair_slots(by_lane, ids_row[...])
    out = refs[-1]
    row = lax.broadcasted_iota(I32, (out.shape[0], by_lane.shape[1]), 0)
    place = placements(row, by_lane * GROUP, slot)
    source = refs[-2][...]
    if scaled:
        source = source.astype(F32)
        mix = refs[0][...]
        pairs = [(mix[:, k : k + 1] * source).astype(BF16) for k in range(2)]
    else:
        pairs = [source, source]
    write_blocks(out, place, jnp.concatenate(pairs, axis=0))


def static_slots(axis, shape):
    index = lax.broadcasted_iota(I32, shape, axis)
    owner = (index * 43) >> 7
    return owner * GROUP, index - owner * CAP


def collect_body(*refs):
    halves = []
    for own, right, left in (refs[0:3], refs[3:6]):
        total = own[...].astype(F32) + right[...].astype(F32) + left[...].astype(F32)
        halves.append(total.astype(BF16))
    rows, out = jnp.concatenate(halves, axis=1), refs[6]
    shape = (out.shape[0], rows.shape[0])
    base, slot = static_slots(1, shape)
    write_blocks(out, placements(lax.broadcasted_iota(I32, shape, 0), base, slot), rows)


def unpack_body(block, *outs):
    count, cols = outs[0].shape
    shape = (count, block.shape[0])
    base, slot = static_slots(0, shape)
    place = placements(lax.broadcasted_iota(I32, shape, 1), base, slot)
    rows = read_blocks(len(outs) * cols, place, block[...])
    for i, out in enumerate(outs):
        out[...] = rows[:, i * cols : (i + 1) * cols]


def combine_body(weighted, ids_lane, ids_row, *refs):
    block, out = refs[-2], refs[-1]
    by_row = ids_row[...]
    _, slot = pair_slots(ids_lane[...], by_row)
    shape = (by_row.shape[0], block.shape[0])
    place = placements(lax.broadcasted_iota(I32, shape, 1), by_row * GROUP, slot)
    count = out.shape[0]
    if weighted:
        mix = refs[0][...]
        split = []
        for p in place:
            weight = p[:count].astype(F32) * mix[:, 0:1] + p[count:].astype(F32) * mix[:, 1:2]
            pieces = []
            for _ in range(3):
                pieces.append(weight.astype(BF16))
                weight = weight - pieces[-1].astype(F32)
            split.append(jnp.concatenate(pieces, axis=0))
        out[...] = read_blocks(out.shape[1], split, block[...], 3)
    else:
        out[...] = read_blocks(out.shape[1], [p[:count] + p[count:] for p in place], block[...])


def single(body, shape, flops, *args, outs=None):
    moved = sum(a.size * a.dtype.itemsize for a in args) + 2 * shape[0] * shape[1] * (outs or 1)
    out_shape = jax.ShapeDtypeStruct(shape, BF16)
    return pl.pallas_call(
        body, out_shape=[out_shape] * outs if outs else out_shape, cost_estimate=cost(flops, moved)
    )(*args)


def per_device(tokens, expert_ids, mix_weights, w_up, w_down, out_grad):
    tok_count, width = tokens.shape
    dp_count = lax.axis_size("dp")
    ring = dp_count // 2
    experts = lax.axis_size("expert") * w_up.shape[0]
    block_shape = (experts * GROUP, block_width(width))
    half_shape = (experts * CAP, width // 2)
    small = 2 * block_shape[0] * block_shape[1] * 256
    core_perm = [(i, i ^ 1) for i in range(dp_count)]

    def shift(value, step):
        perm = [(2 * x + c, 2 * ((x + step) % ring) + c) for x in range(ring) for c in range(2)]
        return lax.ppermute(value, "dp", perm)

    def swap(value):
        return lax.ppermute(value, "dp", core_perm)

    def exchange(packed):
        blocks = packed.reshape(experts, GROUP, block_shape[1])
        moved = lax.all_to_all(blocks, "expert", split_axis=0, concat_axis=0, tiled=True)
        return moved.reshape(block_shape)

    def small_call(body, shape, *args, outs=None):
        return single(body, shape, small, *args, outs=outs)

    def gather_x(low, high):
        right, left = shift(low, 1), shift(high, -1)
        right_high, left_low = shift(high, 1), shift(low, -1)
        far_low, far_high = shift(right, 1), shift(left, -1)
        return (low, high), (right, right_high), (left_low, left), (far_low, far_high)

    def gather_whole(own):
        right, left = shift(own, 1), shift(own, -1)
        far_low = shift(right[:, : width // 2], 1)
        far_high = shift(left[:, width // 2 :], -1)
        return (own,), (right,), (left,), (far_low, far_high)

    def scatter_x(parts):
        low, high, to_left, to_left_high, to_right, to_right_high, far_low, far_high = parts
        via_low, via_high = shift(far_low, 1), shift(far_high, -1)
        high_in, low_in = shift(to_right_high, 1), shift(to_left, -1)
        on_right = (to_right.astype(F32) + via_low.astype(F32)).astype(BF16)
        on_left = (to_left_high.astype(F32) + via_high.astype(F32)).astype(BF16)
        low_other = shift(on_right, 1)
        high_other = shift(on_left, -1)
        return low, low_in, low_other, high, high_in, high_other

    up_own, down_own = w_up[0], w_down[0]
    by_choice = expert_ids.T
    ids_lane, ids_row = by_choice.reshape(1, -1), by_choice.reshape(-1, 1)

    token_send = small_call(
        functools.partial(dispatch_body, False), block_shape, ids_lane, ids_row, tokens)
    token_moved = exchange(token_send)
    grad_send = small_call(
        functools.partial(dispatch_body, True), block_shape,
        ids_lane, ids_row, mix_weights, out_grad)
    grad_moved = exchange(grad_send)

    up_other, down_other = swap(up_own), swap(down_own)
    token_own = small_call(unpack_body, (half_shape[0], width), token_moved)
    grad_own = small_call(unpack_body, half_shape, grad_moved, outs=2)
    token_parts = gather_whole(token_own)
    grad_parts = gather_x(*grad_own)

    token_rows, pre_act, h_own, h_other = rows_matmul(
        token_parts, up_own, up_other, None, STEPS)
    out_parts = project(h_own, h_other, down_own, down_other, False, STEPS)
    grad_rows, p_own, p_other = rows_matmul(
        grad_parts, down_own, down_other, pre_act, STEPS)
    in_parts = project(p_own, p_other, up_own, up_other, True, STEPS)

    out_send = small_call(collect_body, block_shape, *scatter_x(out_parts))
    in_send = small_call(collect_body, block_shape, *scatter_x(in_parts))
    out_back = exchange(out_send)
    in_back = exchange(in_send)

    h_in, g_in = swap(h_other), swap(grad_rows)
    p_in, t_in = swap(p_other), swap(token_rows)
    grad_down = down_grad(h_own, h_in, grad_rows, g_in, STEPS)
    grad_up = up_grad(token_rows, t_in, p_own, p_in, STEPS)

    layer_out = small_call(
        functools.partial(combine_body, True), (tok_count, width),
        ids_lane, ids_row, mix_weights, out_back)
    token_grad = small_call(
        functools.partial(combine_body, False), (tok_count, width),
        ids_lane, ids_row, in_back)
    return layer_out, token_grad, grad_up[None], grad_down[None]


def solution(mesh):
    rows = P(("dp", "expert"), None)
    up, down = P("expert", None, "dp"), P("expert", "dp", None)

    return jax.shard_map(
        per_device,
        mesh=mesh,
        in_specs=(rows, rows, rows, up, down, rows),
        out_specs=(rows, rows, up, down),
        check_vma=False,
    )
```

```python
import functools

import jax
import jax.numpy as jnp
from jax import lax
from jax.experimental import pallas as pl
from jax.experimental.pallas import tpu as pltpu
from jax.sharding import PartitionSpec as P


BF16, F32, I32 = jnp.bfloat16, jnp.float32, jnp.int32
STEPS = 2
CAP = 3
GROUP = 8


def dot(a, b, dims=((1,), (0,))):
    return lax.dot_general(a, b, (dims, ((), ())), preferred_element_type=F32)


def full(shape):
    return pl.BlockSpec(shape, lambda k: (0, 0))


def cost(flops, bytes_accessed):
    return pl.CostEstimate(flops=flops, transcendentals=0, bytes_accessed=bytes_accessed)


def gather_body(back, split, *refs):
    refs, pieces = list(refs), []
    for halves in split:
        pieces.append([refs.pop(0) for _ in range(halves)])
    w_own, w_other = refs[:2]
    if back:
        pre, hidden, rows_out, first, second, acc = refs[2:]
    else:
        rows_out, pre_out, first, second, acc = refs[2:]
    k = pl.program_id(0)
    size = pieces[0][0].shape[0]
    for b, piece in enumerate(pieces):
        for step in range(len(piece)):

            @pl.when((k == step) | (len(piece) == 1))
            def _():
                rows_out[b * size : (b + 1) * size, :] = piece[step][...]

    if back:
        weight = jnp.concatenate([w_own[...], w_other[...]], axis=0)
        part = dot(rows_out[...], weight, ((1,), (1,)))
    else:
        weight = jnp.concatenate([w_own[...], w_other[...]], axis=1)
        part = dot(rows_out[...], weight)

    @pl.when(k == 0)
    def _():
        acc[...] = part

    @pl.when(k > 0)
    def _():
        acc[...] += part

    @pl.when(k == pl.num_programs(0) - 1)
    def _():
        units = first.shape[1]
        if back:
            pre_act = pre[...]
            squash = jax.nn.sigmoid(pre_act)
            value = (acc[...] * (squash * (1.0 + pre_act * (1.0 - squash)))).astype(BF16)
        else:
            pre_act = acc[...]
            pre_out[...] = pre_act
            value = (pre_act * jax.nn.sigmoid(pre_act)).astype(BF16)
        first[...] = value[:, :units]
        if back:
            count = value.shape[0]
            second[:count, :] = hidden[...]
            second[count:, :] = value[:, units:]
        else:
            second[...] = value[:, units:]


def rows_matmul(pieces, w_own, w_other, saved, steps):
    back = len(saved) > 0
    split = tuple(len(piece) for piece in pieces)
    size, cols = pieces[-1][0].shape
    rows, width = 4 * size, cols * steps
    units = w_own.shape[0] if back else w_own.shape[1]
    whole, half = pl.BlockSpec((size, cols), lambda k: (0, k)), full((size, cols))
    piece_specs = [half if n > 1 else whole for n in split for _ in range(n)]
    weight = pl.BlockSpec((units, cols), lambda k: (0, k)) if back else pl.BlockSpec((cols, units), lambda k: (k, 0))
    wide, narrow = full((rows, 2 * units)), full((rows, units))
    other_shape = (2 * rows if back else rows, units)
    small_shapes = [jax.ShapeDtypeStruct(shape, BF16) for shape in ((rows, units), other_shape)]
    return pl.pallas_call(
        functools.partial(gather_body, back, split),
        grid=(steps,),
        in_specs=piece_specs + [weight, weight] + [wide, narrow] * back,
        out_specs=[pl.BlockSpec((rows, cols), lambda k: (0, k))] + [wide] * (not back)
        + [narrow, full(other_shape)],
        out_shape=[jax.ShapeDtypeStruct((rows, width), BF16)]
        + [jax.ShapeDtypeStruct((rows, 2 * units), F32)] * (not back) + small_shapes,
        scratch_shapes=[pltpu.VMEM((rows, 2 * units), F32)],
        cost_estimate=cost(4 * rows * width * units, 4 * (rows * width + width * units)),
    )(*[part for piece in pieces for part in piece], w_own, w_other, *saved)


def project_body(by_rows, h_own, h_other, w_own, w_other, *outs):
    hidden = jnp.concatenate([h_own[...], h_other[...]], axis=1)
    if by_rows:
        weight = jnp.concatenate([w_own[...], w_other[...]], axis=1)
        value = dot(hidden, weight, ((1,), (1,))).astype(BF16)
    else:
        weight = jnp.concatenate([w_own[...], w_other[...]], axis=0)
        value = dot(hidden, weight).astype(BF16)
    size = outs[0].shape[0]
    for step in range(2):

        @pl.when(pl.program_id(0) == step)
        def _():
            for b in range(4):
                outs[2 * b + step][...] = value[b * size : (b + 1) * size, :]


def project(h_own, h_other, w_own, w_other, by_rows, steps, row_block=0):
    rows, units = h_own.shape
    width = w_own.shape[0] if by_rows else w_own.shape[1]
    cols, size = width // steps, rows // 4
    if by_rows:
        weight = pl.BlockSpec((cols, units), lambda k: (k, 0))
    else:
        weight = pl.BlockSpec((units, cols), lambda k: (0, k))
    return pl.pallas_call(
        functools.partial(project_body, by_rows),
        grid=(steps,),
        in_specs=[full((rows, units)), pl.BlockSpec((rows, units), lambda k: (row_block, 0)), weight, weight],
        out_specs=[full((size, cols))] * 8,
        out_shape=[jax.ShapeDtypeStruct((size, cols), BF16)] * 8,
        cost_estimate=cost(4 * rows * width * units, 2 * (rows * width + 2 * width * units)),
    )(h_own, h_other, w_own, w_other)


def down_grad_body(h_a, h_b, g_a, g_b, out):
    hidden = jnp.concatenate([h_a[...], h_b[...]], axis=0)
    rows = jnp.concatenate([g_a[...], g_b[...]], axis=0)
    out[...] = dot(hidden, rows, ((0,), (0,))).astype(BF16)


def down_grad(h_a, h_b, g_a, g_b, steps):
    rows, units = h_a.shape
    width = g_a.shape[1]
    cols = width // steps
    g_spec = pl.BlockSpec((rows, cols), lambda k: (0, k))
    return pl.pallas_call(
        down_grad_body,
        grid=(steps,),
        in_specs=[full((rows, units))] * 2 + [g_spec, g_spec],
        out_specs=pl.BlockSpec((units, cols), lambda k: (0, k)),
        out_shape=jax.ShapeDtypeStruct((units, width), BF16),
        cost_estimate=cost(4 * rows * width * units, 2 * (2 * rows * width + width * units)),
        name="wgrad_down",
    )(h_a, h_b, g_a, g_b)


def up_grad_body(t_a, t_b, p_a, p_b, out):
    rows = jnp.concatenate([t_a[...], t_b[...]], axis=0)
    pre = jnp.concatenate([p_a[...], p_b[...]], axis=0)
    out[...] = dot(rows, pre, ((0,), (0,))).astype(BF16)


def up_grad(t_a, t_b, p_a, p_b, steps):
    rows, units = p_a.shape
    width = t_a.shape[1]
    cols = width // steps
    t_spec = pl.BlockSpec((rows, cols), lambda k: (0, k))
    return pl.pallas_call(
        up_grad_body,
        grid=(steps,),
        in_specs=[t_spec, t_spec, full((rows, units)), pl.BlockSpec((rows, units), lambda k: (1, 0))],
        out_specs=pl.BlockSpec((cols, units), lambda k: (k, 0)),
        out_shape=jax.ShapeDtypeStruct((width, units), BF16),
        cost_estimate=cost(4 * rows * width * units, 2 * (2 * rows * width + width * units)),
        name="wgrad_up",
    )(t_a, t_b, p_a, p_b)


def sizes(width):
    rest = 6 * (width // 28)
    return (width - rest) // 2, rest


def block_width(width):
    return sizes(width)[0]


def placements(row, base, slot):
    main = [row == base + 2 * slot, row == base + 2 * slot + 1]
    rest = ((slot == 0) & (row == base + 6)) | ((slot == 1) & (row == base + 7))
    last = [(slot == 2) & (row == base + 6), (slot == 2) & (row == base + 7)]
    return [hit.astype(BF16) for hit in (main[0], main[1], rest, last[0], last[1])]


def write_blocks(out, place, rows):
    wide, rest = sizes(rows.shape[1])
    half, start = rest // 2, 2 * wide
    lead = jnp.concatenate(place[:3], axis=1)
    second = jnp.concatenate(place[:2] + place[3:], axis=1)
    third = jnp.concatenate(place[:2], axis=1)
    out[:, :rest] = dot(lead, jnp.concatenate(
        [rows[:, :rest], rows[:, wide : wide + rest], rows[:, start:]], axis=0)).astype(BF16)
    end = rest + half
    out[:, rest:end] = dot(second, jnp.concatenate(
        [rows[:, rest:end], rows[:, wide + rest : wide + end],
         rows[:, start : start + half], rows[:, start + half :]], axis=0)).astype(BF16)
    out[:, end:] = dot(third, jnp.concatenate(
        [rows[:, end:wide], rows[:, wide + end : start]], axis=0)).astype(BF16)


def read_blocks(width, place, block, parts=1):
    _, rest = sizes(width)
    half = rest // 2

    def pick(a, b):
        value = dot(a, b)
        size = value.shape[0] // parts
        total = value[(parts - 1) * size :]
        for part in range(parts - 2, -1, -1):
            total = total + value[part * size : (part + 1) * size]
        return total.astype(BF16)

    both = jnp.concatenate([place[2], place[3]], axis=1)
    other = jnp.concatenate([place[2], place[4]], axis=1)
    side = block[:, rest : rest + half]
    return jnp.concatenate(
        [
            pick(place[0], block),
            pick(place[1], block),
            pick(both, jnp.concatenate([block[:, :half], side], axis=0)),
            pick(other, jnp.concatenate([block[:, half:rest], side], axis=0)),
        ],
        axis=1,
    )


def pair_slots(ids):
    by_row = jnp.concatenate([ids[:, 0:1], ids[:, 1:2]], axis=0)
    count = by_row.shape[0]
    first = lax.broadcasted_iota(I32, (count, count), 0)
    second = lax.broadcasted_iota(I32, (count, count), 1)
    wide = jnp.broadcast_to(by_row.astype(F32), (count, count))
    by_lane = jnp.sum(jnp.where(first == second, wide, 0.0), axis=0, keepdims=True)
    same = wide == by_lane
    along_lane = jnp.sum((same & (first < second)).astype(F32), axis=0, keepdims=True)
    along_row = jnp.sum((same & (second < first)).astype(F32), axis=1, keepdims=True)
    return by_lane.astype(I32), along_lane.astype(I32), by_row, along_row.astype(I32)


def dispatch_body(scaled, ids, *refs):
    by_lane, slot, _, _ = pair_slots(ids[...])
    out = refs[-1]
    row = lax.broadcasted_iota(I32, (out.shape[0], by_lane.shape[1]), 0)
    place = placements(row, by_lane * GROUP, slot)
    source = refs[-2][...]
    if scaled:
        source = source.astype(F32)
        mix = refs[0][...]
        pairs = [(mix[:, k : k + 1] * source).astype(BF16) for k in range(2)]
    else:
        pairs = [source, source]
    write_blocks(out, place, jnp.concatenate(pairs, axis=0))


def static_slots(axis, shape):
    index = lax.broadcasted_iota(I32, shape, axis)
    owner = (index * 43) >> 7
    return owner * GROUP, index - owner * CAP


def collect_body(*refs):
    halves = []
    for own, right, left in (refs[0:3], refs[3:6]):
        total = own[...].astype(F32) + right[...].astype(F32) + left[...].astype(F32)
        halves.append(total.astype(BF16))
    rows, out = jnp.concatenate(halves, axis=1), refs[6]
    shape = (out.shape[0], rows.shape[0])
    base, slot = static_slots(1, shape)
    write_blocks(out, placements(lax.broadcasted_iota(I32, shape, 0), base, slot), rows)


def relay_body(first, first_via, second, second_via, first_out, second_out):
    first_out[...] = (first[...].astype(F32) + first_via[...].astype(F32)).astype(BF16)
    second_out[...] = (second[...].astype(F32) + second_via[...].astype(F32)).astype(BF16)


def unpack_body(block, *outs):
    count, cols = outs[0].shape
    shape = (count, block.shape[0])
    base, slot = static_slots(0, shape)
    place = placements(lax.broadcasted_iota(I32, shape, 1), base, slot)
    rows = read_blocks(len(outs) * cols, place, block[...])
    for i, out in enumerate(outs):
        out[...] = rows[:, i * cols : (i + 1) * cols]


def combine_body(weighted, ids, *refs):
    block, out = refs[-2], refs[-1]
    _, _, by_row, slot = pair_slots(ids[...])
    shape = (by_row.shape[0], block.shape[0])
    place = placements(lax.broadcasted_iota(I32, shape, 1), by_row * GROUP, slot)
    count = out.shape[0]
    if weighted:
        mix = refs[0][...]
        split = []
        for p in place:
            weight = p[:count].astype(F32) * mix[:, 0:1] + p[count:].astype(F32) * mix[:, 1:2]
            pieces = []
            for _ in range(3):
                pieces.append(weight.astype(BF16))
                weight = weight - pieces[-1].astype(F32)
            split.append(jnp.concatenate(pieces, axis=0))
        out[...] = read_blocks(out.shape[1], split, block[...], 3)
    else:
        out[...] = read_blocks(out.shape[1], [p[:count] + p[count:] for p in place], block[...])


def single(body, shape, flops, *args, outs=None):
    moved = sum(a.size * a.dtype.itemsize for a in args) + 2 * shape[0] * shape[1] * (outs or 1)
    out_shape = jax.ShapeDtypeStruct(shape, BF16)
    return pl.pallas_call(
        body, out_shape=[out_shape] * outs if outs else out_shape, cost_estimate=cost(flops, moved)
    )(*args)


def per_device(tokens, expert_ids, mix_weights, w_up, w_down, out_grad):
    tok_count, width = tokens.shape
    dp_count = lax.axis_size("dp")
    ring = dp_count // 2
    experts = lax.axis_size("expert") * w_up.shape[0]
    block_shape = (experts * GROUP, block_width(width))
    half_shape = (experts * CAP, width // 2)
    small = 2 * block_shape[0] * block_shape[1] * 256
    core_perm = [(i, i ^ 1) for i in range(dp_count)]

    def shift(value, step):
        perm = [(2 * x + c, 2 * ((x + step) % ring) + c) for x in range(ring) for c in range(2)]
        return lax.ppermute(value, "dp", perm)

    def swap(value):
        return lax.ppermute(value, "dp", core_perm)

    def exchange(packed):
        blocks = packed.reshape(experts, GROUP, block_shape[1])
        moved = lax.all_to_all(blocks, "expert", split_axis=0, concat_axis=0, tiled=True)
        return moved.reshape(block_shape)

    def small_call(body, shape, *args, outs=None):
        return single(body, shape, small, *args, outs=outs)

    def gather_x(low, high):
        right, left = shift(low, 1), shift(high, -1)
        right_high, left_low = shift(high, 1), shift(low, -1)
        far_low, far_high = shift(right, 1), shift(left, -1)
        return (low, high), (right, right_high), (left_low, left), (far_low, far_high)

    def scatter_x(parts):
        low, high, to_left, to_left_high, to_right, to_right_high, far_low, far_high = parts
        via_low, via_high = shift(far_low, 1), shift(far_high, -1)
        high_in, low_in = shift(to_right_high, 1), shift(to_left, -1)
        on_right, on_left = small_call(
            relay_body, half_shape, to_right, via_low, to_left_high, via_high,
            outs=2)
        low_other = shift(on_right, 1)
        high_other = shift(on_left, -1)
        return low, low_in, low_other, high, high_in, high_other

    up_own, down_own = w_up[0], w_down[0]

    token_send = small_call(
        functools.partial(dispatch_body, False), block_shape, expert_ids, tokens)
    token_moved = exchange(token_send)
    grad_send = small_call(
        functools.partial(dispatch_body, True), block_shape,
        expert_ids, mix_weights, out_grad)
    grad_moved = exchange(grad_send)

    up_other, down_other = swap(up_own), swap(down_own)
    token_own = small_call(unpack_body, half_shape, token_moved, outs=2)
    grad_own = small_call(unpack_body, half_shape, grad_moved, outs=2)
    token_parts = gather_x(*token_own)
    grad_parts = gather_x(*grad_own)

    token_rows, pre_act, h_own, h_other = rows_matmul(
        token_parts, up_own, up_other, (), STEPS)
    out_parts = project(h_own, h_other, down_own, down_other, False, STEPS)
    grad_rows, p_own, both_other = rows_matmul(
        grad_parts, down_own, down_other, (pre_act, h_other), STEPS)

    in_parts = project(p_own, both_other, up_own, up_other, True, STEPS, 1)

    out_send = small_call(collect_body, block_shape, *scatter_x(out_parts))
    in_send = small_call(collect_body, block_shape, *scatter_x(in_parts))
    out_back = exchange(out_send)
    in_back = exchange(in_send)

    both_in = swap(both_other)
    g_in, t_in = swap(grad_rows), swap(token_rows)
    grad_down = down_grad(h_own, both_in, grad_rows, g_in, 2 * STEPS)
    grad_up = up_grad(token_rows, t_in, p_own, both_in, 2 * STEPS)

    layer_out = small_call(
        functools.partial(combine_body, True), (tok_count, width),
        expert_ids, mix_weights, out_back)
    token_grad = small_call(
        functools.partial(combine_body, False), (tok_count, width),
        expert_ids, in_back)
    return layer_out, token_grad, grad_up[None], grad_down[None]


def solution(mesh):
    rows = P(("dp", "expert"), None)
    up, down = P("expert", None, "dp"), P("expert", "dp", None)

    return jax.shard_map(
        per_device,
        mesh=mesh,
        in_specs=(rows, rows, rows, up, down, rows),
        out_specs=(rows, rows, up, down),
        check_vma=False,
    )
```

```python
import functools

import jax
import jax.numpy as jnp
from jax import lax
from jax.experimental import pallas as pl
from jax.experimental.pallas import tpu as pltpu
from jax.sharding import PartitionSpec as P


BF16, F32, I32 = jnp.bfloat16, jnp.float32, jnp.int32
STEPS = 2
CAP = 3
GROUP = 8


def dot(a, b, dims=((1,), (0,))):
    return lax.dot_general(a, b, (dims, ((), ())), preferred_element_type=F32)


def full(shape):
    return pl.BlockSpec(shape, lambda k: (0, 0))


def cost(flops, bytes_accessed):
    return pl.CostEstimate(flops=flops, transcendentals=0, bytes_accessed=bytes_accessed)


def layer_body(back, *refs):
    refs = list(refs)
    take = lambda n: [refs.pop(0) for _ in range(n)]
    pieces, (up_own, up_other, down_own, down_other) = take(8), take(4)
    if back:
        pre_in, hidden_in = take(2)
        rows_out, own_out, other_out = take(3)
    else:
        rows_out, pre_out, own_out, other_out = take(4)
    parts = take(8)
    rows, up, down, pre, acc, own, other, result, sems = refs
    size, half = pieces[0].shape
    count, _ = rows.shape
    units = up_own.shape[1]
    used = []

    def copy(source, target):
        used.append(None)
        return pltpu.make_async_copy(source, target, sems.at[len(used) - 1])

    def begin(tasks):
        for task in tasks:
            task.start()

    def finish(tasks):
        for task in tasks:
            task.wait()

    def columns(k):
        return slice(k * half, (k + 1) * half)

    up_tasks, down_tasks, row_tasks, part_tasks = [], [], [], []
    for k in range(2):
        cols = columns(k)
        up_tasks.append([
            copy(up_own.at[cols, :], up.at[cols, :units]),
            copy(up_other.at[cols, :], up.at[cols, units:])])
        down_tasks.append([
            copy(down_own.at[:, cols], down.at[:units, cols]),
            copy(down_other.at[:, cols], down.at[units:, cols])])
        blocks = [slice(b * size, (b + 1) * size) for b in range(4)]
        row_tasks.append([
            copy(pieces[2 * b + k], rows.at[block, cols]) for b, block in enumerate(blocks)])
        part_tasks.append([
            copy(result.at[block, cols], parts[2 * b + k]) for b, block in enumerate(blocks)])
    first_tasks, second_tasks = (down_tasks, up_tasks) if back else (up_tasks, down_tasks)
    rows_task = copy(rows, rows_out)
    own_task = copy(own, own_out)
    other_task = copy(other, other_out.at[count:, :] if back else other_out)
    if back:
        extra = [copy(pre_in, pre), copy(hidden_in, other_out.at[:count, :])]
    else:
        extra = [copy(acc, pre_out)]

    begin(row_tasks[0] + first_tasks[0] + row_tasks[1] + first_tasks[1])
    if back:
        begin(extra)

    def first_half(k, carry):
        @pl.when(k == 0)
        def _():
            finish(row_tasks[0] + first_tasks[0])

        @pl.when(k == 1)
        def _():
            finish(row_tasks[1] + first_tasks[1])
            rows_task.start()
            begin(second_tasks[0] + second_tasks[1])

        at = pl.ds(pl.multiple_of(k * half, 128), half)
        if back:
            value = dot(rows[:, at], down[:, at], ((1,), (1,)))
        else:
            value = dot(rows[:, at], up[at, :])

        @pl.when(k == 0)
        def _():
            acc[...] = value

        @pl.when(k == 1)
        def _():
            acc[...] += value

        return carry

    lax.fori_loop(0, 2, first_half, 0)
    total = acc[...]
    if back:
        extra[0].wait()
        pre_act = pre[...]
        squash = jax.nn.sigmoid(pre_act)
        active = (total * (squash * (1.0 + pre_act * (1.0 - squash)))).astype(BF16)
    else:
        begin(extra)
        active = (total * jax.nn.sigmoid(total)).astype(BF16)
    own[...] = active[:, :units]
    other[...] = active[:, units:]
    begin([own_task, other_task])

    def second_half(k, carry):
        @pl.when(k == 0)
        def _():
            finish(second_tasks[0])

        @pl.when(k == 1)
        def _():
            finish(second_tasks[1])

        at = pl.ds(pl.multiple_of(k * half, 128), half)
        both = jnp.concatenate([own[...], other[...]], axis=1)
        if back:
            value = dot(both, up[at, :], ((1,), (1,)))
        else:
            value = dot(both, down[:, at])
        result[:, at] = value.astype(BF16)

        @pl.when(k == 0)
        def _():
            begin(part_tasks[0])

        @pl.when(k == 1)
        def _():
            begin(part_tasks[1])

        return carry

    lax.fori_loop(0, 2, second_half, 0)
    finish([rows_task, own_task, other_task] + (extra[1:] if back else extra))
    finish(part_tasks[0] + part_tasks[1])


def layer_call(pieces, weights, saved):
    back = len(saved) > 0
    size, half = pieces[0].shape
    rows, width = 4 * size, 2 * half
    units = weights[0].shape[1]
    shape = jax.ShapeDtypeStruct
    outs = [shape((rows, width), BF16)]
    if not back:
        outs.append(shape((rows, 2 * units), F32))
    outs += [shape((rows, units), BF16), shape((2 * rows if back else rows, units), BF16)]
    outs += [shape((size, half), BF16)] * 8
    anywhere = pl.BlockSpec(memory_space=pl.ANY)
    return pl.pallas_call(
        functools.partial(layer_body, back),
        in_specs=[anywhere] * (12 + len(saved)),
        out_specs=[anywhere] * len(outs),
        out_shape=outs,
        scratch_shapes=[
            pltpu.VMEM((rows, width), BF16),
            pltpu.VMEM((width, 2 * units), BF16),
            pltpu.VMEM((2 * units, width), BF16),
            pltpu.VMEM((rows, 2 * units), F32),
            pltpu.VMEM((rows, 2 * units), F32),
            pltpu.VMEM((rows, units), BF16),
            pltpu.VMEM((rows, units), BF16),
            pltpu.VMEM((rows, width), BF16),
            pltpu.SemaphoreType.DMA((48,)),
        ],
        cost_estimate=cost(8 * rows * width * units, 6 * rows * width + 8 * width * units),
    )(*pieces, *weights, *saved)


def down_grad_body(h_a, h_b, g_a, g_b, out):
    hidden = jnp.concatenate([h_a[...], h_b[...]], axis=0)
    rows = jnp.concatenate([g_a[...], g_b[...]], axis=0)
    out[...] = dot(hidden, rows, ((0,), (0,))).astype(BF16)


def down_grad(h_a, h_b, g_a, g_b, steps):
    rows, units = h_a.shape
    width = g_a.shape[1]
    cols = width // steps
    g_spec = pl.BlockSpec((rows, cols), lambda k: (0, k))
    return pl.pallas_call(
        down_grad_body,
        grid=(steps,),
        in_specs=[full((rows, units))] * 2 + [g_spec, g_spec],
        out_specs=pl.BlockSpec((units, cols), lambda k: (0, k)),
        out_shape=jax.ShapeDtypeStruct((units, width), BF16),
        cost_estimate=cost(4 * rows * width * units, 2 * (2 * rows * width + width * units)),
        name="wgrad_down",
    )(h_a, h_b, g_a, g_b)


def up_grad_body(t_a, t_b, p_a, p_b, out):
    rows = jnp.concatenate([t_a[...], t_b[...]], axis=0)
    pre = jnp.concatenate([p_a[...], p_b[...]], axis=0)
    out[...] = dot(rows, pre, ((0,), (0,))).astype(BF16)


def up_grad(t_a, t_b, p_a, p_b, steps):
    rows, units = p_a.shape
    width = t_a.shape[1]
    cols = width // steps
    t_spec = pl.BlockSpec((rows, cols), lambda k: (0, k))
    return pl.pallas_call(
        up_grad_body,
        grid=(steps,),
        in_specs=[t_spec, t_spec, full((rows, units)), pl.BlockSpec((rows, units), lambda k: (1, 0))],
        out_specs=pl.BlockSpec((cols, units), lambda k: (k, 0)),
        out_shape=jax.ShapeDtypeStruct((width, units), BF16),
        cost_estimate=cost(4 * rows * width * units, 2 * (2 * rows * width + width * units)),
        name="wgrad_up",
    )(t_a, t_b, p_a, p_b)


def sizes(width):
    rest = 6 * (width // 28)
    return (width - rest) // 2, rest


def block_width(width):
    return sizes(width)[0]


def placements(row, base, slot):
    main = [row == base + 2 * slot, row == base + 2 * slot + 1]
    rest = ((slot == 0) & (row == base + 6)) | ((slot == 1) & (row == base + 7))
    last = [(slot == 2) & (row == base + 6), (slot == 2) & (row == base + 7)]
    return [hit.astype(BF16) for hit in (main[0], main[1], rest, last[0], last[1])]


def write_blocks(out, place, rows):
    wide, rest = sizes(rows.shape[1])
    half, start = rest // 2, 2 * wide
    lead = jnp.concatenate(place[:3], axis=1)
    second = jnp.concatenate(place[:2] + place[3:], axis=1)
    third = jnp.concatenate(place[:2], axis=1)
    out[:, :rest] = dot(lead, jnp.concatenate(
        [rows[:, :rest], rows[:, wide : wide + rest], rows[:, start:]], axis=0)).astype(BF16)
    end = rest + half
    out[:, rest:end] = dot(second, jnp.concatenate(
        [rows[:, rest:end], rows[:, wide + rest : wide + end],
         rows[:, start : start + half], rows[:, start + half :]], axis=0)).astype(BF16)
    out[:, end:] = dot(third, jnp.concatenate(
        [rows[:, end:wide], rows[:, wide + end : start]], axis=0)).astype(BF16)


def read_blocks(width, place, block, parts=1):
    _, rest = sizes(width)
    half = rest // 2

    def pick(a, b):
        value = dot(a, b)
        size = value.shape[0] // parts
        total = value[(parts - 1) * size :]
        for part in range(parts - 2, -1, -1):
            total = total + value[part * size : (part + 1) * size]
        return total.astype(BF16)

    both = jnp.concatenate([place[2], place[3]], axis=1)
    other = jnp.concatenate([place[2], place[4]], axis=1)
    side = block[:, rest : rest + half]
    return jnp.concatenate(
        [
            pick(place[0], block),
            pick(place[1], block),
            pick(both, jnp.concatenate([block[:, :half], side], axis=0)),
            pick(other, jnp.concatenate([block[:, half:rest], side], axis=0)),
        ],
        axis=1,
    )


def pair_slots(ids):
    by_row = jnp.concatenate([ids[:, 0:1], ids[:, 1:2]], axis=0)
    count = by_row.shape[0]
    first = lax.broadcasted_iota(I32, (count, count), 0)
    second = lax.broadcasted_iota(I32, (count, count), 1)
    wide = jnp.broadcast_to(by_row.astype(F32), (count, count))
    by_lane = jnp.sum(jnp.where(first == second, wide, 0.0), axis=0, keepdims=True)
    same = wide == by_lane
    along_lane = jnp.sum((same & (first < second)).astype(F32), axis=0, keepdims=True)
    along_row = jnp.sum((same & (second < first)).astype(F32), axis=1, keepdims=True)
    return by_lane.astype(I32), along_lane.astype(I32), by_row, along_row.astype(I32)


def dispatch_body(scaled, ids, *refs):
    by_lane, slot, _, _ = pair_slots(ids[...])
    out = refs[-1]
    row = lax.broadcasted_iota(I32, (out.shape[0], by_lane.shape[1]), 0)
    place = placements(row, by_lane * GROUP, slot)
    source = refs[-2][...]
    if scaled:
        source = source.astype(F32)
        mix = refs[0][...]
        pairs = [(mix[:, k : k + 1] * source).astype(BF16) for k in range(2)]
    else:
        pairs = [source, source]
    write_blocks(out, place, jnp.concatenate(pairs, axis=0))


def static_slots(axis, shape):
    index = lax.broadcasted_iota(I32, shape, axis)
    owner = (index * 43) >> 7
    return owner * GROUP, index - owner * CAP


def collect_body(*refs):
    halves = []
    for own, right, left in (refs[0:3], refs[3:6]):
        total = own[...].astype(F32) + right[...].astype(F32) + left[...].astype(F32)
        halves.append(total.astype(BF16))
    rows, out = jnp.concatenate(halves, axis=1), refs[6]
    shape = (out.shape[0], rows.shape[0])
    base, slot = static_slots(1, shape)
    write_blocks(out, placements(lax.broadcasted_iota(I32, shape, 0), base, slot), rows)


def relay_body(first, first_via, second, second_via, first_out, second_out):
    first_out[...] = (first[...].astype(F32) + first_via[...].astype(F32)).astype(BF16)
    second_out[...] = (second[...].astype(F32) + second_via[...].astype(F32)).astype(BF16)


def unpack_body(block, *outs):
    count, cols = outs[0].shape
    shape = (count, block.shape[0])
    base, slot = static_slots(0, shape)
    place = placements(lax.broadcasted_iota(I32, shape, 1), base, slot)
    rows = read_blocks(len(outs) * cols, place, block[...])
    for i, out in enumerate(outs):
        out[...] = rows[:, i * cols : (i + 1) * cols]


def combine_body(weighted, ids, *refs):
    block, out = refs[-2], refs[-1]
    _, _, by_row, slot = pair_slots(ids[...])
    shape = (by_row.shape[0], block.shape[0])
    place = placements(lax.broadcasted_iota(I32, shape, 1), by_row * GROUP, slot)
    count = out.shape[0]
    if weighted:
        mix = refs[0][...]
        split = []
        for p in place:
            weight = p[:count].astype(F32) * mix[:, 0:1] + p[count:].astype(F32) * mix[:, 1:2]
            pieces = []
            for _ in range(3):
                pieces.append(weight.astype(BF16))
                weight = weight - pieces[-1].astype(F32)
            split.append(jnp.concatenate(pieces, axis=0))
        out[...] = read_blocks(out.shape[1], split, block[...], 3)
    else:
        out[...] = read_blocks(out.shape[1], [p[:count] + p[count:] for p in place], block[...])


def single(body, shape, flops, *args, outs=None):
    moved = sum(a.size * a.dtype.itemsize for a in args) + 2 * shape[0] * shape[1] * (outs or 1)
    out_shape = jax.ShapeDtypeStruct(shape, BF16)
    return pl.pallas_call(
        body, out_shape=[out_shape] * outs if outs else out_shape, cost_estimate=cost(flops, moved)
    )(*args)


def per_device(tokens, expert_ids, mix_weights, w_up, w_down, out_grad):
    tok_count, width = tokens.shape
    dp_count = lax.axis_size("dp")
    ring = dp_count // 2
    experts = lax.axis_size("expert") * w_up.shape[0]
    block_shape = (experts * GROUP, block_width(width))
    half_shape = (experts * CAP, width // 2)
    small = 2 * block_shape[0] * block_shape[1] * 256
    core_perm = [(i, i ^ 1) for i in range(dp_count)]

    def shift(value, step):
        perm = [(2 * x + c, 2 * ((x + step) % ring) + c) for x in range(ring) for c in range(2)]
        return lax.ppermute(value, "dp", perm)

    def swap(value):
        return lax.ppermute(value, "dp", core_perm)

    def exchange(packed):
        blocks = packed.reshape(experts, GROUP, block_shape[1])
        moved = lax.all_to_all(blocks, "expert", split_axis=0, concat_axis=0, tiled=True)
        return moved.reshape(block_shape)

    def small_call(body, shape, *args, outs=None):
        return single(body, shape, small, *args, outs=outs)

    def gather_x(low, high):
        right, left = shift(low, 1), shift(high, -1)
        right_high, left_low = shift(high, 1), shift(low, -1)
        far_low, far_high = shift(right, 1), shift(left, -1)
        return low, high, right, right_high, left_low, left, far_low, far_high

    def scatter_x(parts):
        low, high, to_left, to_left_high, to_right, to_right_high, far_low, far_high = parts
        via_low, via_high = shift(far_low, 1), shift(far_high, -1)
        high_in, low_in = shift(to_right_high, 1), shift(to_left, -1)
        on_right, on_left = small_call(
            relay_body, half_shape, to_right, via_low, to_left_high, via_high,
            outs=2)
        low_other = shift(on_right, 1)
        high_other = shift(on_left, -1)
        return low, low_in, low_other, high, high_in, high_other

    up_own, down_own = w_up[0], w_down[0]

    token_send = small_call(
        functools.partial(dispatch_body, False), block_shape, expert_ids, tokens)
    token_moved = exchange(token_send)
    grad_send = small_call(
        functools.partial(dispatch_body, True), block_shape,
        expert_ids, mix_weights, out_grad)
    grad_moved = exchange(grad_send)

    up_other, down_other = swap(up_own), swap(down_own)
    token_own = small_call(unpack_body, half_shape, token_moved, outs=2)
    grad_own = small_call(unpack_body, half_shape, grad_moved, outs=2)
    token_parts = gather_x(*token_own)
    grad_parts = gather_x(*grad_own)

    weights = up_own, up_other, down_own, down_other
    token_rows, pre_act, h_own, h_other, *out_parts = layer_call(
        token_parts, weights, ())
    grad_rows, p_own, both_other, *in_parts = layer_call(
        grad_parts, weights, (pre_act, h_other))

    out_send = small_call(collect_body, block_shape, *scatter_x(out_parts))
    in_send = small_call(collect_body, block_shape, *scatter_x(in_parts))
    out_back = exchange(out_send)
    in_back = exchange(in_send)

    both_in = swap(both_other)
    g_in, t_in = swap(grad_rows), swap(token_rows)
    grad_down = down_grad(h_own, both_in, grad_rows, g_in, 2 * STEPS)
    grad_up = up_grad(token_rows, t_in, p_own, both_in, 2 * STEPS)

    layer_out = small_call(
        functools.partial(combine_body, True), (tok_count, width),
        expert_ids, mix_weights, out_back)
    token_grad = small_call(
        functools.partial(combine_body, False), (tok_count, width),
        expert_ids, in_back)
    return layer_out, token_grad, grad_up[None], grad_down[None]


def solution(mesh):
    rows = P(("dp", "expert"), None)
    up, down = P("expert", None, "dp"), P("expert", "dp", None)

    return jax.shard_map(
        per_device,
        mesh=mesh,
        in_specs=(rows, rows, rows, up, down, rows),
        out_specs=(rows, rows, up, down),
        check_vma=False,
    )
```

```python
import functools

import jax
import jax.numpy as jnp
from jax import lax
from jax.experimental import pallas as pl
from jax.experimental.pallas import tpu as pltpu
from jax.sharding import PartitionSpec as P


BF16, F32, I32 = jnp.bfloat16, jnp.float32, jnp.int32
STEPS = 2
CAP = 3
GROUP = 8


def dot(a, b, dims=((1,), (0,))):
    return lax.dot_general(a, b, (dims, ((), ())), preferred_element_type=F32)


def full(shape):
    return pl.BlockSpec(shape, lambda k: (0, 0))


def cost(flops, bytes_accessed):
    return pl.CostEstimate(flops=flops, transcendentals=0, bytes_accessed=bytes_accessed)


def layer_body(back, *refs):
    refs = list(refs)
    take = lambda n: [refs.pop(0) for _ in range(n)]
    pieces, (up_own, up_other, down_own, down_other) = take(8), take(4)
    if back:
        pre_in, hidden_in = take(2)
        rows_out, own_out, other_out = take(3)
    else:
        rows_out, pre_out, own_out, other_out = take(4)
    parts = take(8)
    rows, up, down, pre, acc, own, other, result, sems = refs
    size, half = pieces[0].shape
    count, _ = rows.shape
    units = up_own.shape[1]
    used = []

    def copy(source, target):
        used.append(None)
        return pltpu.make_async_copy(source, target, sems.at[len(used) - 1])

    def begin(tasks):
        for task in tasks:
            task.start()

    def finish(tasks):
        for task in tasks:
            task.wait()

    def columns(k):
        return slice(k * half, (k + 1) * half)

    up_tasks, down_tasks, row_tasks, part_tasks = [], [], [], []
    for k in range(2):
        cols = columns(k)
        up_tasks.append([
            copy(up_own.at[cols, :], up.at[cols, :units]),
            copy(up_other.at[cols, :], up.at[cols, units:])])
        down_tasks.append([
            copy(down_own.at[:, cols], down.at[:units, cols]),
            copy(down_other.at[:, cols], down.at[units:, cols])])
        blocks = [slice(b * size, (b + 1) * size) for b in range(4)]
        row_tasks.append([
            copy(pieces[2 * b + k], rows.at[block, cols]) for b, block in enumerate(blocks)])
        part_tasks.append([
            copy(result.at[block, cols], parts[2 * b + k]) for b, block in enumerate(blocks)])
    first_tasks, second_tasks = (down_tasks, up_tasks) if back else (up_tasks, down_tasks)
    rows_task = copy(rows, rows_out)
    own_task = copy(own, own_out)
    other_task = copy(other, other_out.at[count:, :] if back else other_out)
    if back:
        extra = [copy(pre_in, pre), copy(hidden_in, other_out.at[:count, :])]
    else:
        extra = [copy(acc, pre_out)]

    begin(row_tasks[0] + first_tasks[0] + row_tasks[1] + first_tasks[1])
    if back:
        begin(extra)

    def first_half(k, carry):
        @pl.when(k == 0)
        def _():
            finish(row_tasks[0] + first_tasks[0])

        @pl.when(k == 1)
        def _():
            finish(row_tasks[1] + first_tasks[1])
            rows_task.start()
            begin(second_tasks[0] + second_tasks[1])

        at = pl.ds(pl.multiple_of(k * half, 128), half)
        if back:
            value = dot(rows[:, at], down[:, at], ((1,), (1,)))
        else:
            value = dot(rows[:, at], up[at, :])

        @pl.when(k == 0)
        def _():
            acc[...] = value

        @pl.when(k == 1)
        def _():
            acc[...] += value

        return carry

    lax.fori_loop(0, 2, first_half, 0)
    total = acc[...]
    if back:
        extra[0].wait()
        pre_act = pre[...]
        squash = jax.nn.sigmoid(pre_act)
        active = (total * (squash * (1.0 + pre_act * (1.0 - squash)))).astype(BF16)
    else:
        begin(extra)
        active = (total * jax.nn.sigmoid(total)).astype(BF16)
    own[...] = active[:, :units]
    other[...] = active[:, units:]
    begin([own_task, other_task])

    def second_half(k, carry):
        @pl.when(k == 0)
        def _():
            finish(second_tasks[0])

        @pl.when(k == 1)
        def _():
            finish(second_tasks[1])

        at = pl.ds(pl.multiple_of(k * half, 128), half)
        both = jnp.concatenate([own[...], other[...]], axis=1)
        if back:
            value = dot(both, up[at, :], ((1,), (1,)))
        else:
            value = dot(both, down[:, at])
        result[:, at] = value.astype(BF16)

        @pl.when(k == 0)
        def _():
            begin(part_tasks[0])

        @pl.when(k == 1)
        def _():
            begin(part_tasks[1])

        return carry

    lax.fori_loop(0, 2, second_half, 0)
    finish([rows_task, own_task, other_task] + (extra[1:] if back else extra))
    finish(part_tasks[0] + part_tasks[1])


def layer_call(pieces, weights, saved):
    back = len(saved) > 0
    size, half = pieces[0].shape
    rows, width = 4 * size, 2 * half
    units = weights[0].shape[1]
    shape = jax.ShapeDtypeStruct
    outs = [shape((rows, width), BF16)]
    if not back:
        outs.append(shape((rows, 2 * units), F32))
    outs += [shape((rows, units), BF16), shape((2 * rows if back else rows, units), BF16)]
    outs += [shape((size, half), BF16)] * 8
    anywhere = pl.BlockSpec(memory_space=pl.ANY)
    return pl.pallas_call(
        functools.partial(layer_body, back),
        in_specs=[anywhere] * (12 + len(saved)),
        out_specs=[anywhere] * len(outs),
        out_shape=outs,
        scratch_shapes=[
            pltpu.VMEM((rows, width), BF16),
            pltpu.VMEM((width, 2 * units), BF16),
            pltpu.VMEM((2 * units, width), BF16),
            pltpu.VMEM((rows, 2 * units), F32),
            pltpu.VMEM((rows, 2 * units), F32),
            pltpu.VMEM((rows, units), BF16),
            pltpu.VMEM((rows, units), BF16),
            pltpu.VMEM((rows, width), BF16),
            pltpu.SemaphoreType.DMA((48,)),
        ],
        compiler_params=pltpu.CompilerParams(vmem_limit_bytes=28 * 2**20),
        cost_estimate=cost(8 * rows * width * units, 6 * rows * width + 8 * width * units),
    )(*pieces, *weights, *saved)


def down_grad_body(h_a, h_b, g_a, g_b, out):
    hidden = jnp.concatenate([h_a[...], h_b[...]], axis=0)
    rows = jnp.concatenate([g_a[...], g_b[...]], axis=0)
    out[...] = dot(hidden, rows, ((0,), (0,))).astype(BF16)


def down_grad(h_a, h_b, g_a, g_b, steps):
    rows, units = h_a.shape
    width = g_a.shape[1]
    cols = width // steps
    g_spec = pl.BlockSpec((rows, cols), lambda k: (0, k))
    return pl.pallas_call(
        down_grad_body,
        grid=(steps,),
        in_specs=[full((rows, units))] * 2 + [g_spec, g_spec],
        out_specs=pl.BlockSpec((units, cols), lambda k: (0, k)),
        out_shape=jax.ShapeDtypeStruct((units, width), BF16),
        compiler_params=pltpu.CompilerParams(vmem_limit_bytes=12 * 2**20),
        cost_estimate=cost(4 * rows * width * units, 2 * (2 * rows * width + width * units)),
        name="wgrad_down",
    )(h_a, h_b, g_a, g_b)


def up_grad_body(t_a, t_b, p_a, p_b, out):
    rows = jnp.concatenate([t_a[...], t_b[...]], axis=0)
    pre = jnp.concatenate([p_a[...], p_b[...]], axis=0)
    out[...] = dot(rows, pre, ((0,), (0,))).astype(BF16)


def up_grad(t_a, t_b, p_a, p_b, steps):
    rows, units = p_a.shape
    width = t_a.shape[1]
    cols = width // steps
    t_spec = pl.BlockSpec((rows, cols), lambda k: (0, k))
    return pl.pallas_call(
        up_grad_body,
        grid=(steps,),
        in_specs=[t_spec, t_spec, full((rows, units)), pl.BlockSpec((rows, units), lambda k: (1, 0))],
        out_specs=pl.BlockSpec((cols, units), lambda k: (k, 0)),
        out_shape=jax.ShapeDtypeStruct((width, units), BF16),
        compiler_params=pltpu.CompilerParams(vmem_limit_bytes=12 * 2**20),
        cost_estimate=cost(4 * rows * width * units, 2 * (2 * rows * width + width * units)),
        name="wgrad_up",
    )(t_a, t_b, p_a, p_b)


def sizes(width):
    rest = 6 * (width // 28)
    return (width - rest) // 2, rest


def block_width(width):
    return sizes(width)[0]


def placements(row, base, slot):
    main = [row == base + 2 * slot, row == base + 2 * slot + 1]
    rest = ((slot == 0) & (row == base + 6)) | ((slot == 1) & (row == base + 7))
    last = [(slot == 2) & (row == base + 6), (slot == 2) & (row == base + 7)]
    return [hit.astype(BF16) for hit in (main[0], main[1], rest, last[0], last[1])]


def write_blocks(out, place, rows):
    wide, rest = sizes(rows.shape[1])
    half, start = rest // 2, 2 * wide
    lead = jnp.concatenate(place[:3], axis=1)
    second = jnp.concatenate(place[:2] + place[3:], axis=1)
    third = jnp.concatenate(place[:2], axis=1)
    out[:, :rest] = dot(lead, jnp.concatenate(
        [rows[:, :rest], rows[:, wide : wide + rest], rows[:, start:]], axis=0)).astype(BF16)
    end = rest + half
    out[:, rest:end] = dot(second, jnp.concatenate(
        [rows[:, rest:end], rows[:, wide + rest : wide + end],
         rows[:, start : start + half], rows[:, start + half :]], axis=0)).astype(BF16)
    out[:, end:] = dot(third, jnp.concatenate(
        [rows[:, end:wide], rows[:, wide + end : start]], axis=0)).astype(BF16)


def read_blocks(width, place, block, parts=1):
    _, rest = sizes(width)
    half = rest // 2

    def pick(a, b):
        value = dot(a, b)
        size = value.shape[0] // parts
        total = value[(parts - 1) * size :]
        for part in range(parts - 2, -1, -1):
            total = total + value[part * size : (part + 1) * size]
        return total.astype(BF16)

    both = jnp.concatenate([place[2], place[3]], axis=1)
    other = jnp.concatenate([place[2], place[4]], axis=1)
    side = block[:, rest : rest + half]
    return jnp.concatenate(
        [
            pick(place[0], block),
            pick(place[1], block),
            pick(both, jnp.concatenate([block[:, :half], side], axis=0)),
            pick(other, jnp.concatenate([block[:, half:rest], side], axis=0)),
        ],
        axis=1,
    )


def to_rows(by_lane):
    count = by_lane.shape[1]
    first = lax.broadcasted_iota(I32, (count, count), 0)
    second = lax.broadcasted_iota(I32, (count, count), 1)
    wide = jnp.broadcast_to(by_lane, (count, count))
    return jnp.sum(jnp.where(first == second, wide, 0.0), axis=1, keepdims=True)


def pair_slots(ids):
    by_lane = jnp.concatenate([ids[0:1, :], ids[1:2, :]], axis=1).astype(F32)
    by_row = to_rows(by_lane)
    count = by_row.shape[0]
    first = lax.broadcasted_iota(I32, (count, count), 0)
    second = lax.broadcasted_iota(I32, (count, count), 1)
    same = by_row == by_lane
    along_lane = jnp.sum((same & (first < second)).astype(F32), axis=0, keepdims=True)
    along_row = jnp.sum((same & (second < first)).astype(F32), axis=1, keepdims=True)
    return tuple(v.astype(I32) for v in (by_lane, along_lane, by_row, along_row))


def dispatch_body(scaled, ids, *refs):
    by_lane, slot, _, _ = pair_slots(ids[...])
    out = refs[-1]
    row = lax.broadcasted_iota(I32, (out.shape[0], by_lane.shape[1]), 0)
    place = placements(row, by_lane * GROUP, slot)
    source = refs[-2][...]
    if scaled:
        source = source.astype(F32)
        mix = refs[0][...]
        pairs = [(to_rows(mix[k : k + 1, :]) * source).astype(BF16) for k in range(2)]
    else:
        pairs = [source, source]
    write_blocks(out, place, jnp.concatenate(pairs, axis=0))


def static_slots(axis, shape):
    index = lax.broadcasted_iota(I32, shape, axis)
    owner = (index * 43) >> 7
    return owner * GROUP, index - owner * CAP


def collect_body(*refs):
    halves = []
    for own, right, left in (refs[0:3], refs[3:6]):
        total = own[...].astype(F32) + right[...].astype(F32) + left[...].astype(F32)
        halves.append(total.astype(BF16))
    rows, out = jnp.concatenate(halves, axis=1), refs[6]
    shape = (out.shape[0], rows.shape[0])
    base, slot = static_slots(1, shape)
    write_blocks(out, placements(lax.broadcasted_iota(I32, shape, 0), base, slot), rows)


def relay_body(first, first_via, second, second_via, first_out, second_out):
    first_out[...] = (first[...].astype(F32) + first_via[...].astype(F32)).astype(BF16)
    second_out[...] = (second[...].astype(F32) + second_via[...].astype(F32)).astype(BF16)


def unpack_body(block, *outs):
    count, cols = outs[0].shape
    shape = (count, block.shape[0])
    base, slot = static_slots(0, shape)
    place = placements(lax.broadcasted_iota(I32, shape, 1), base, slot)
    rows = read_blocks(len(outs) * cols, place, block[...])
    for i, out in enumerate(outs):
        out[...] = rows[:, i * cols : (i + 1) * cols]


def combine_body(weighted, ids, *refs):
    block, out = refs[-2], refs[-1]
    _, _, by_row, slot = pair_slots(ids[...])
    shape = (by_row.shape[0], block.shape[0])
    place = placements(lax.broadcasted_iota(I32, shape, 1), by_row * GROUP, slot)
    count = out.shape[0]
    if weighted:
        mix = refs[0][...]
        first_mix, second_mix = to_rows(mix[0:1, :]), to_rows(mix[1:2, :])
        split = []
        for p in place:
            weight = p[:count].astype(F32) * first_mix + p[count:].astype(F32) * second_mix
            pieces = []
            for _ in range(3):
                pieces.append(weight.astype(BF16))
                weight = weight - pieces[-1].astype(F32)
            split.append(jnp.concatenate(pieces, axis=0))
        out[...] = read_blocks(out.shape[1], split, block[...], 3)
    else:
        out[...] = read_blocks(out.shape[1], [p[:count] + p[count:] for p in place], block[...])


def single(body, shape, flops, *args, outs=None):
    moved = sum(a.size * a.dtype.itemsize for a in args) + 2 * shape[0] * shape[1] * (outs or 1)
    out_shape = jax.ShapeDtypeStruct(shape, BF16)
    return pl.pallas_call(
        body,
        in_specs=[pl.BlockSpec(memory_space=pltpu.VMEM)] * len(args),
        out_shape=[out_shape] * outs if outs else out_shape,
        compiler_params=pltpu.CompilerParams(vmem_limit_bytes=12 * 2**20),
        cost_estimate=cost(flops, moved),
    )(*args)


def per_device(tokens, expert_ids, mix_weights, w_up, w_down, out_grad):
    tok_count, width = tokens.shape
    dp_count = lax.axis_size("dp")
    ring = dp_count // 2
    experts = lax.axis_size("expert") * w_up.shape[0]
    block_shape = (experts * GROUP, block_width(width))
    half_shape = (experts * CAP, width // 2)
    small = 2 * block_shape[0] * block_shape[1] * 256
    core_perm = [(i, i ^ 1) for i in range(dp_count)]

    def shift(value, step):
        perm = [(2 * x + c, 2 * ((x + step) % ring) + c) for x in range(ring) for c in range(2)]
        return lax.ppermute(value, "dp", perm)

    def swap(value):
        return lax.ppermute(value, "dp", core_perm)

    def exchange(packed):
        blocks = packed.reshape(experts, GROUP, block_shape[1])
        moved = lax.all_to_all(blocks, "expert", split_axis=0, concat_axis=0, tiled=True)
        return moved.reshape(block_shape)

    def small_call(body, shape, *args, outs=None):
        return single(body, shape, small, *args, outs=outs)

    def gather_x(low, high):
        right, left = shift(low, 1), shift(high, -1)
        right_high, left_low = shift(high, 1), shift(low, -1)
        far_low, far_high = shift(right, 1), shift(left, -1)
        return low, high, right, right_high, left_low, left, far_low, far_high

    def scatter_x(parts):
        low, high, to_left, to_left_high, to_right, to_right_high, far_low, far_high = parts
        via_low, via_high = shift(far_low, 1), shift(far_high, -1)
        high_in, low_in = shift(to_right_high, 1), shift(to_left, -1)
        on_right, on_left = small_call(
            relay_body, half_shape, to_right, via_low, to_left_high, via_high,
            outs=2)
        low_other = shift(on_right, 1)
        high_other = shift(on_left, -1)
        return low, low_in, low_other, high, high_in, high_other

    up_own, down_own = w_up[0], w_down[0]
    ids, mix = expert_ids.T, mix_weights.T

    token_send = small_call(
        functools.partial(dispatch_body, False), block_shape, ids, tokens)
    token_moved = exchange(token_send)
    grad_send = small_call(
        functools.partial(dispatch_body, True), block_shape,
        ids, mix, out_grad)
    grad_moved = exchange(grad_send)

    up_other, down_other = swap(up_own), swap(down_own)
    token_own = small_call(unpack_body, half_shape, token_moved, outs=2)
    grad_own = small_call(unpack_body, half_shape, grad_moved, outs=2)
    token_parts = gather_x(*token_own)
    grad_parts = gather_x(*grad_own)

    weights = up_own, up_other, down_own, down_other
    token_rows, pre_act, h_own, h_other, *out_parts = layer_call(
        token_parts, weights, ())
    grad_rows, p_own, both_other, *in_parts = layer_call(
        grad_parts, weights, (pre_act, h_other))

    out_send = small_call(collect_body, block_shape, *scatter_x(out_parts))
    in_send = small_call(collect_body, block_shape, *scatter_x(in_parts))
    out_back = exchange(out_send)
    in_back = exchange(in_send)

    both_in = swap(both_other)
    g_in, t_in = swap(grad_rows), swap(token_rows)
    grad_down = down_grad(h_own, both_in, grad_rows, g_in, 2 * STEPS)
    grad_up = up_grad(token_rows, t_in, p_own, both_in, 2 * STEPS)

    layer_out = small_call(
        functools.partial(combine_body, True), (tok_count, width),
        ids, mix, out_back)
    token_grad = small_call(
        functools.partial(combine_body, False), (tok_count, width),
        ids, in_back)
    return layer_out, token_grad, grad_up[None], grad_down[None]


def solution(mesh):
    rows = P(("dp", "expert"), None)
    up, down = P("expert", None, "dp"), P("expert", "dp", None)

    return jax.shard_map(
        per_device,
        mesh=mesh,
        in_specs=(rows, rows, rows, up, down, rows),
        out_specs=(rows, rows, up, down),
        check_vma=False,
    )
```

```python
import functools

import jax
import jax.numpy as jnp
from jax import lax
from jax.experimental import pallas as pl
from jax.experimental.pallas import tpu as pltpu
from jax.sharding import PartitionSpec as P


BF16, F32, I32 = jnp.bfloat16, jnp.float32, jnp.int32
STEPS = 2
CAP = 3
GROUP = 8


def dot(a, b, dims=((1,), (0,))):
    return lax.dot_general(a, b, (dims, ((), ())), preferred_element_type=F32)


def full(shape):
    return pl.BlockSpec(shape, lambda k: (0, 0))


def cost(flops, bytes_accessed):
    return pl.CostEstimate(flops=flops, transcendentals=0, bytes_accessed=bytes_accessed)


def layer_body(back, *refs):
    refs = list(refs)
    take = lambda n: [refs.pop(0) for _ in range(n)]
    pieces, (up_own, up_other, down_own, down_other) = take(8), take(4)
    if back:
        pre_in, hidden_in = take(2)
        rows_out, own_out, other_out = take(3)
    else:
        rows_out, pre_out, own_out, other_out = take(4)
    parts = take(8)
    rows, up, down, pre, acc, own, other, result, sems = refs
    size, half = pieces[0].shape
    count, _ = rows.shape
    units = up_own.shape[1]
    used = []

    def copy(source, target):
        used.append(None)
        return pltpu.make_async_copy(source, target, sems.at[len(used) - 1])

    def begin(tasks):
        for task in tasks:
            task.start()

    def finish(tasks):
        for task in tasks:
            task.wait()

    def columns(k):
        return slice(k * half, (k + 1) * half)

    up_tasks, down_tasks, row_tasks, part_tasks = [], [], [], []
    for k in range(2):
        cols = columns(k)
        up_tasks.append([
            copy(up_own.at[cols, :], up.at[cols, :units]),
            copy(up_other.at[cols, :], up.at[cols, units:])])
        down_tasks.append([
            copy(down_own.at[:, cols], down.at[:units, cols]),
            copy(down_other.at[:, cols], down.at[units:, cols])])
        blocks = [slice(b * size, (b + 1) * size) for b in range(4)]
        row_tasks.append([
            copy(pieces[2 * b + k], rows.at[block, cols]) for b, block in enumerate(blocks)])
        part_tasks.append([
            copy(result.at[block, cols], parts[2 * b + k]) for b, block in enumerate(blocks)])
    first_tasks, second_tasks = (down_tasks, up_tasks) if back else (up_tasks, down_tasks)
    rows_task = copy(rows, rows_out)
    own_task = copy(own, own_out)
    other_task = copy(other, other_out.at[count:, :] if back else other_out)
    if back:
        extra = [copy(pre_in, pre), copy(hidden_in, other_out.at[:count, :])]
    else:
        extra = [copy(acc, pre_out)]

    begin(row_tasks[0] + first_tasks[0] + row_tasks[1] + first_tasks[1])
    if back:
        begin(extra)

    def first_half(k, carry):
        @pl.when(k == 0)
        def _():
            finish(row_tasks[0] + first_tasks[0])

        @pl.when(k == 1)
        def _():
            finish(row_tasks[1] + first_tasks[1])
            rows_task.start()
            begin(second_tasks[0] + second_tasks[1])

        at = pl.ds(pl.multiple_of(k * half, 128), half)
        if back:
            value = dot(rows[:, at], down[:, at], ((1,), (1,)))
        else:
            value = dot(rows[:, at], up[at, :])

        @pl.when(k == 0)
        def _():
            acc[...] = value

        @pl.when(k == 1)
        def _():
            acc[...] += value

        return carry

    lax.fori_loop(0, 2, first_half, 0)
    total = acc[...]
    if back:
        extra[0].wait()
        pre_act = pre[...]
        squash = jax.nn.sigmoid(pre_act)
        active = (total * (squash * (1.0 + pre_act * (1.0 - squash)))).astype(BF16)
    else:
        begin(extra)
        active = (total * jax.nn.sigmoid(total)).astype(BF16)
    own[...] = active[:, :units]
    other[...] = active[:, units:]
    begin([own_task, other_task])

    def second_half(k, carry):
        @pl.when(k == 0)
        def _():
            finish(second_tasks[0])

        @pl.when(k == 1)
        def _():
            finish(second_tasks[1])

        at = pl.ds(pl.multiple_of(k * half, 128), half)
        both = jnp.concatenate([own[...], other[...]], axis=1)
        if back:
            value = dot(both, up[at, :], ((1,), (1,)))
        else:
            value = dot(both, down[:, at])
        result[:, at] = value.astype(BF16)

        @pl.when(k == 0)
        def _():
            begin(part_tasks[0])

        @pl.when(k == 1)
        def _():
            begin(part_tasks[1])

        return carry

    lax.fori_loop(0, 2, second_half, 0)
    finish([rows_task, own_task, other_task] + (extra[1:] if back else extra))
    finish(part_tasks[0] + part_tasks[1])


def layer_call(pieces, weights, saved):
    back = len(saved) > 0
    size, half = pieces[0].shape
    rows, width = 4 * size, 2 * half
    units = weights[0].shape[1]
    shape = jax.ShapeDtypeStruct
    outs = [shape((rows, width), BF16)]
    if not back:
        outs.append(shape((rows, 2 * units), F32))
    outs += [shape((rows, units), BF16), shape((2 * rows if back else rows, units), BF16)]
    outs += [shape((size, half), BF16)] * 8
    anywhere = pl.BlockSpec(memory_space=pl.ANY)
    main = pl.BlockSpec(memory_space=pltpu.HBM)
    return pl.pallas_call(
        functools.partial(layer_body, back),
        in_specs=[anywhere] * 8 + [main] * 4 + [anywhere] * len(saved),
        out_specs=[main] + [anywhere] * (not back) + [main] + [anywhere] * 9,
        out_shape=outs,
        scratch_shapes=[
            pltpu.VMEM((rows, width), BF16),
            pltpu.VMEM((width, 2 * units), BF16),
            pltpu.VMEM((2 * units, width), BF16),
            pltpu.VMEM((rows, 2 * units), F32),
            pltpu.VMEM((rows, 2 * units), F32),
            pltpu.VMEM((rows, units), BF16),
            pltpu.VMEM((rows, units), BF16),
            pltpu.VMEM((rows, width), BF16),
            pltpu.SemaphoreType.DMA((48,)),
        ],
        compiler_params=pltpu.CompilerParams(vmem_limit_bytes=28 * 2**20),
        cost_estimate=cost(8 * rows * width * units, 6 * rows * width + 8 * width * units),
    )(*pieces, *map(in_hbm, weights), *saved)


def down_grad_body(h_a, h_b, g_a, g_b, out):
    hidden = jnp.concatenate([h_a[...], h_b[...]], axis=0)
    rows = jnp.concatenate([g_a[...], g_b[...]], axis=0)
    out[...] = dot(hidden, rows, ((0,), (0,))).astype(BF16)


def down_grad(h_a, h_b, g_a, g_b, steps):
    rows, units = h_a.shape
    width = g_a.shape[1]
    cols = width // steps
    g_spec = pl.BlockSpec((rows, cols), lambda k: (0, k))
    return pl.pallas_call(
        down_grad_body,
        grid=(steps,),
        in_specs=[full((rows, units))] * 2 + [g_spec, g_spec],
        out_specs=pl.BlockSpec((units, cols), lambda k: (0, k)),
        out_shape=jax.ShapeDtypeStruct((units, width), BF16),
        compiler_params=pltpu.CompilerParams(vmem_limit_bytes=12 * 2**20),
        cost_estimate=cost(4 * rows * width * units, 2 * (2 * rows * width + width * units)),
        name="wgrad_down",
    )(h_a, h_b, g_a, g_b)


def up_grad_body(t_a, t_b, p_a, p_b, out):
    rows = jnp.concatenate([t_a[...], t_b[...]], axis=0)
    pre = jnp.concatenate([p_a[...], p_b[...]], axis=0)
    out[...] = dot(rows, pre, ((0,), (0,))).astype(BF16)


def up_grad(t_a, t_b, p_a, p_b, steps):
    rows, units = p_a.shape
    width = t_a.shape[1]
    cols = width // steps
    t_spec = pl.BlockSpec((rows, cols), lambda k: (0, k))
    return pl.pallas_call(
        up_grad_body,
        grid=(steps,),
        in_specs=[t_spec, t_spec, full((rows, units)), pl.BlockSpec((rows, units), lambda k: (1, 0))],
        out_specs=pl.BlockSpec((cols, units), lambda k: (k, 0)),
        out_shape=jax.ShapeDtypeStruct((width, units), BF16),
        compiler_params=pltpu.CompilerParams(vmem_limit_bytes=12 * 2**20),
        cost_estimate=cost(4 * rows * width * units, 2 * (2 * rows * width + width * units)),
        name="wgrad_up",
    )(t_a, t_b, p_a, p_b)


def sizes(width):
    rest = 6 * (width // 28)
    return (width - rest) // 2, rest


def block_width(width):
    return sizes(width)[0]


def placements(row, base, slot):
    main = [row == base + 2 * slot, row == base + 2 * slot + 1]
    rest = ((slot == 0) & (row == base + 6)) | ((slot == 1) & (row == base + 7))
    last = [(slot == 2) & (row == base + 6), (slot == 2) & (row == base + 7)]
    return [hit.astype(BF16) for hit in (main[0], main[1], rest, last[0], last[1])]


def write_blocks(out, place, rows):
    wide, rest = sizes(rows.shape[1])
    half, start = rest // 2, 2 * wide
    lead = jnp.concatenate(place[:3], axis=1)
    second = jnp.concatenate(place[:2] + place[3:], axis=1)
    third = jnp.concatenate(place[:2], axis=1)
    out[:, :rest] = dot(lead, jnp.concatenate(
        [rows[:, :rest], rows[:, wide : wide + rest], rows[:, start:]], axis=0)).astype(BF16)
    end = rest + half
    out[:, rest:end] = dot(second, jnp.concatenate(
        [rows[:, rest:end], rows[:, wide + rest : wide + end],
         rows[:, start : start + half], rows[:, start + half :]], axis=0)).astype(BF16)
    out[:, end:] = dot(third, jnp.concatenate(
        [rows[:, end:wide], rows[:, wide + end : start]], axis=0)).astype(BF16)


def read_blocks(width, place, block, parts=1):
    _, rest = sizes(width)
    half = rest // 2

    def pick(a, b):
        value = dot(a, b)
        size = value.shape[0] // parts
        total = value[(parts - 1) * size :]
        for part in range(parts - 2, -1, -1):
            total = total + value[part * size : (part + 1) * size]
        return total.astype(BF16)

    both = jnp.concatenate([place[2], place[3]], axis=1)
    other = jnp.concatenate([place[2], place[4]], axis=1)
    side = block[:, rest : rest + half]
    return jnp.concatenate(
        [
            pick(place[0], block),
            pick(place[1], block),
            pick(both, jnp.concatenate([block[:, :half], side], axis=0)),
            pick(other, jnp.concatenate([block[:, half:rest], side], axis=0)),
        ],
        axis=1,
    )


def to_rows(by_lane):
    count = by_lane.shape[1]
    first = lax.broadcasted_iota(I32, (count, count), 0)
    second = lax.broadcasted_iota(I32, (count, count), 1)
    wide = jnp.broadcast_to(by_lane, (count, count))
    return jnp.sum(jnp.where(first == second, wide, 0.0), axis=1, keepdims=True)


def pair_slots(ids):
    by_lane = jnp.concatenate([ids[0:1, :], ids[1:2, :]], axis=1).astype(F32)
    by_row = to_rows(by_lane)
    count = by_row.shape[0]
    first = lax.broadcasted_iota(I32, (count, count), 0)
    second = lax.broadcasted_iota(I32, (count, count), 1)
    same = by_row == by_lane
    along_lane = jnp.sum((same & (first < second)).astype(F32), axis=0, keepdims=True)
    along_row = jnp.sum((same & (second < first)).astype(F32), axis=1, keepdims=True)
    return tuple(v.astype(I32) for v in (by_lane, along_lane, by_row, along_row))


def dispatch_body(scaled, ids, *refs):
    by_lane, slot, _, _ = pair_slots(ids[...])
    out = refs[-1]
    row = lax.broadcasted_iota(I32, (out.shape[0], by_lane.shape[1]), 0)
    place = placements(row, by_lane * GROUP, slot)
    source = refs[-2][...]
    if scaled:
        source = source.astype(F32)
        mix = refs[0][...]
        pairs = [(to_rows(mix[k : k + 1, :]) * source).astype(BF16) for k in range(2)]
    else:
        pairs = [source, source]
    write_blocks(out, place, jnp.concatenate(pairs, axis=0))


def static_slots(axis, shape):
    index = lax.broadcasted_iota(I32, shape, axis)
    owner = (index * 43) >> 7
    return owner * GROUP, index - owner * CAP


def collect_body(*refs):
    halves = []
    for own, right, left in (refs[0:3], refs[3:6]):
        total = own[...].astype(F32) + right[...].astype(F32) + left[...].astype(F32)
        halves.append(total.astype(BF16))
    rows, out = jnp.concatenate(halves, axis=1), refs[6]
    shape = (out.shape[0], rows.shape[0])
    base, slot = static_slots(1, shape)
    write_blocks(out, placements(lax.broadcasted_iota(I32, shape, 0), base, slot), rows)


def relay_body(first, first_via, second, second_via, first_out, second_out):
    first_out[...] = (first[...].astype(F32) + first_via[...].astype(F32)).astype(BF16)
    second_out[...] = (second[...].astype(F32) + second_via[...].astype(F32)).astype(BF16)


def unpack_body(block, *outs):
    count, cols = outs[0].shape
    shape = (count, block.shape[0])
    base, slot = static_slots(0, shape)
    place = placements(lax.broadcasted_iota(I32, shape, 1), base, slot)
    rows = read_blocks(len(outs) * cols, place, block[...])
    for i, out in enumerate(outs):
        out[...] = rows[:, i * cols : (i + 1) * cols]


def combine_body(weighted, ids, *refs):
    block, out = refs[-2], refs[-1]
    _, _, by_row, slot = pair_slots(ids[...])
    shape = (by_row.shape[0], block.shape[0])
    place = placements(lax.broadcasted_iota(I32, shape, 1), by_row * GROUP, slot)
    count = out.shape[0]
    if weighted:
        mix = refs[0][...]
        first_mix, second_mix = to_rows(mix[0:1, :]), to_rows(mix[1:2, :])
        split = []
        for p in place:
            weight = p[:count].astype(F32) * first_mix + p[count:].astype(F32) * second_mix
            pieces = []
            for _ in range(3):
                pieces.append(weight.astype(BF16))
                weight = weight - pieces[-1].astype(F32)
            split.append(jnp.concatenate(pieces, axis=0))
        out[...] = read_blocks(out.shape[1], split, block[...], 3)
    else:
        out[...] = read_blocks(out.shape[1], [p[:count] + p[count:] for p in place], block[...])


def fetch_body(body, count, *refs):
    inputs, out = refs[:count], refs[count]
    buffers, sems = refs[count + 1 : -1], refs[-1]
    tasks = [
        pltpu.make_async_copy(source, target, sems.at[i])
        for i, (source, target) in enumerate(zip(inputs, buffers))
    ]
    for task in tasks:
        task.start()
    for task in tasks:
        task.wait()
    body(*buffers, out)


def in_hbm(value):
    return pltpu.with_memory_space_constraint(value, pltpu.HBM)


def fetching(body, shape, flops, *args):
    moved = sum(a.size * a.dtype.itemsize for a in args) + 2 * shape[0] * shape[1]
    return pl.pallas_call(
        functools.partial(fetch_body, body, len(args)),
        in_specs=[pl.BlockSpec(memory_space=pltpu.HBM)] * len(args),
        out_shape=jax.ShapeDtypeStruct(shape, BF16),
        scratch_shapes=[pltpu.VMEM(a.shape, a.dtype) for a in args]
        + [pltpu.SemaphoreType.DMA((len(args),))],
        compiler_params=pltpu.CompilerParams(vmem_limit_bytes=12 * 2**20),
        cost_estimate=cost(flops, moved),
    )(*map(in_hbm, args))


def single(body, shape, flops, *args, outs=None):
    moved = sum(a.size * a.dtype.itemsize for a in args) + 2 * shape[0] * shape[1] * (outs or 1)
    out_shape = jax.ShapeDtypeStruct(shape, BF16)
    return pl.pallas_call(
        body,
        in_specs=[pl.BlockSpec(memory_space=pltpu.VMEM)] * len(args),
        out_shape=[out_shape] * outs if outs else out_shape,
        compiler_params=pltpu.CompilerParams(vmem_limit_bytes=12 * 2**20),
        cost_estimate=cost(flops, moved),
    )(*args)


def per_device(tokens, expert_ids, mix_weights, w_up, w_down, out_grad):
    tok_count, width = tokens.shape
    dp_count = lax.axis_size("dp")
    ring = dp_count // 2
    experts = lax.axis_size("expert") * w_up.shape[0]
    block_shape = (experts * GROUP, block_width(width))
    half_shape = (experts * CAP, width // 2)
    small = 2 * block_shape[0] * block_shape[1] * 256
    core_perm = [(i, i ^ 1) for i in range(dp_count)]

    def shift(value, step):
        perm = [(2 * x + c, 2 * ((x + step) % ring) + c) for x in range(ring) for c in range(2)]
        return lax.ppermute(value, "dp", perm)

    def swap(value):
        return lax.ppermute(value, "dp", core_perm)

    def exchange(packed):
        blocks = packed.reshape(experts, GROUP, block_shape[1])
        moved = lax.all_to_all(blocks, "expert", split_axis=0, concat_axis=0, tiled=True)
        return moved.reshape(block_shape)

    def small_call(body, shape, *args, outs=None):
        return single(body, shape, small, *args, outs=outs)

    def gather_x(low, high):
        right, left = shift(low, 1), shift(high, -1)
        right_high, left_low = shift(high, 1), shift(low, -1)
        far_low, far_high = shift(right, 1), shift(left, -1)
        return low, high, right, right_high, left_low, left, far_low, far_high

    def scatter_x(parts):
        low, high, to_left, to_left_high, to_right, to_right_high, far_low, far_high = parts
        via_low, via_high = shift(far_low, 1), shift(far_high, -1)
        high_in, low_in = shift(to_right_high, 1), shift(to_left, -1)
        on_right, on_left = small_call(
            relay_body, half_shape, to_right, via_low, to_left_high, via_high,
            outs=2)
        low_other = shift(on_right, 1)
        high_other = shift(on_left, -1)
        return low, low_in, low_other, high, high_in, high_other

    up_own, down_own = w_up[0], w_down[0]
    ids, mix = expert_ids.T, mix_weights.T

    token_send = fetching(
        functools.partial(dispatch_body, False), block_shape, small, ids, tokens)
    token_moved = exchange(token_send)
    grad_send = fetching(
        functools.partial(dispatch_body, True), block_shape, small,
        ids, mix, out_grad)
    grad_moved = exchange(grad_send)

    up_other, down_other = swap(up_own), swap(down_own)
    token_own = small_call(unpack_body, half_shape, token_moved, outs=2)
    grad_own = small_call(unpack_body, half_shape, grad_moved, outs=2)
    token_parts = gather_x(*token_own)
    grad_parts = gather_x(*grad_own)

    weights = up_own, up_other, down_own, down_other
    token_rows, pre_act, h_own, h_other, *out_parts = layer_call(
        token_parts, weights, ())
    grad_rows, p_own, both_other, *in_parts = layer_call(
        grad_parts, weights, (pre_act, h_other))

    out_send = small_call(collect_body, block_shape, *scatter_x(out_parts))
    in_send = small_call(collect_body, block_shape, *scatter_x(in_parts))
    out_back = exchange(out_send)
    in_back = exchange(in_send)

    both_in = swap(both_other)
    g_in, t_in = swap(grad_rows), swap(token_rows)
    grad_down = down_grad(in_hbm(h_own), both_in, grad_rows, g_in, 2 * STEPS)
    grad_up = up_grad(token_rows, t_in, in_hbm(p_own), both_in, 2 * STEPS)

    layer_out = small_call(
        functools.partial(combine_body, True), (tok_count, width),
        ids, mix, out_back)
    token_grad = small_call(
        functools.partial(combine_body, False), (tok_count, width),
        ids, in_back)
    return layer_out, token_grad, grad_up[None], grad_down[None]


def solution(mesh):
    rows = P(("dp", "expert"), None)
    up, down = P("expert", None, "dp"), P("expert", "dp", None)

    return jax.shard_map(
        per_device,
        mesh=mesh,
        in_specs=(rows, rows, rows, up, down, rows),
        out_specs=(rows, rows, up, down),
        check_vma=False,
    )
```
